512 devices in a mesh: ctx: 64 (over z, y_hi, core), tp: 8 (over x, y_lo).
Axes of the slice: x: 4, y: 4 (y_hi: 2, y_lo: 2; y = y_hi * 2 + y_lo), z: 16, core: 2. Of those that a mesh axis runs over, the one named last changes fastest.
Arguments:
- queries: bfloat16 [8192, 8192], P('ctx', 'tp'), may hold values from -8 to 8
- keys: bfloat16 [8192, 1024], P('ctx', 'tp'), may hold values from -4 to 4
- values: bfloat16 [8192, 1024], P('ctx', 'tp'), may hold values from -4 to 4
- attn_out: bfloat16 [8192, 8192], P('ctx', 'tp'), may hold values from -4 to 4, as said below
- out_grad: bfloat16 [8192, 8192], P(('ctx', 'tp')), may hold values from -24 to 24
- logsumexp: float32 [64, 8192], P('tp', 'ctx'), may hold values from -50 to 50, as said below
- position_ids: int32 [3, 8192], P(None, 'ctx'), may hold values from 0 to 8191, as said below
- block_map: int32 [128], replicated, may hold values from 0 to 127, as said below
- span_blocks: int32 [16, 2], replicated, may hold values from 0 to 127, as said below
Outputs:
- grad_q: bfloat16 [8192, 8192], P('ctx', 'tp')
- key_gradient: bfloat16 [8192, 1024], P('ctx', 'tp')
- value_gradient: bfloat16 [8192, 1024], P('ctx', 'tp')
The draws below stay inside these ranges and needn't reach their ends.
Inputs may be any that keep to these rules, and one draw needn't show every extreme that they name: `block_map`: a permutation of the sequence blocks. `span_blocks`: spans ascend in sequence order and do not intersect; each row is a start block and an end block past the span's last; the first span starts at block 0 and the last ends at block 127. `position_ids`: given inputs, not renumbered after spans: text rows carry their sequence position in all three ids; a row of a visual span carries the span's first position plus its frame, grid row and grid column. `attn_out`: the output of the forward pass for these queries, keys and values. `logsumexp`: the log of each row's softmax total over its allowed keys, from the forward pass.
All inputs are finite; a program needn't handle non-finite values.
Results may differ from the reference program's by a relative error of at most 0.011.
Values may be sent and summed in bfloat16 or wider, within the bound.
A program may use at most 64 MiB of HBM per device.

```python
import math
import jax
import jax.numpy as jnp
from jax import lax

QUERY_HEADS = 64
KEY_VALUE_HEADS = 8
HEAD_SIZE = 128
BLK = 64
NBLK = 128
SEQUENCE_TOKENS = 8192
SPANS = 16


THETA = 1000000.0


def layout_ints(key):
    permuted = jax.random.permutation(jax.random.fold_in(key, 101), NBLK).astype(jnp.int32)
    segment = NBLK // SPANS
    offsets = jax.random.randint(jax.random.fold_in(key, 102), (SPANS,), 0, 4).astype(jnp.int32)
    offsets = offsets.at[0].set(0)
    raw_bits = jax.random.randint(jax.random.fold_in(key, 103), (SPANS,), 0, 1 << 20).astype(jnp.int32)
    room_left = segment - offsets
    lengths = 1 + raw_bits % (room_left - 1)
    lengths = lengths.at[SPANS - 1].set(room_left[SPANS - 1] - 1)
    starts = jnp.arange(SPANS, dtype=jnp.int32) * segment + offsets
    return (permuted, starts, starts + lengths)


def row_info(key):
    permuted, starts, ends = layout_ints(key)
    row_index = jnp.arange(SEQUENCE_TOKENS, dtype=jnp.int32)
    seq_pos = permuted[row_index // BLK] * BLK + row_index % BLK
    seq_block = seq_pos // BLK
    inside = (seq_block[:, None] >= starts[None, :]) & (seq_block[:, None] < ends[None, :])
    numbers = jnp.arange(SPANS, dtype=jnp.int32)[None, :] + 1
    span_ids = jnp.sum(jnp.where(inside, numbers, 0), axis=1).astype(jnp.int32) - 1
    span_start = jnp.sum(jnp.where(inside, starts[None, :], 0), axis=1).astype(jnp.int32)
    return (seq_pos, span_ids, span_start)


def draw_block_map(key, part):
    return layout_ints(key)[0]


def draw_span_blocks(key, part):
    permuted, starts, ends = layout_ints(key)
    return jnp.stack([starts, ends], axis=1)


def draw_position_ids(key, part):
    seq_pos, span_ids, span_start = row_info(key)
    grid_side = 8 if BLK % 8 == 0 else 2
    base_pos = span_start * BLK
    offset = seq_pos - base_pos
    visual = span_ids >= 0
    temporal = jnp.where(visual, base_pos + offset // BLK, seq_pos)
    height = jnp.where(visual, base_pos + offset % BLK // grid_side, seq_pos)
    width_id = jnp.where(visual, base_pos + offset % grid_side, seq_pos)
    return jnp.stack([temporal, height, width_id]).astype(jnp.int32)


def float_portion(key, salt, shape, spread):
    sub_key = jax.random.fold_in(key, salt)
    values_out = jnp.clip(jax.random.normal(sub_key, shape, jnp.float32) * spread, -4.0 * spread, 4.0 * spread)
    return values_out.astype(jnp.bfloat16)


def draw_queries(key, part):
    return float_portion(key, 201, (SEQUENCE_TOKENS, QUERY_HEADS * HEAD_SIZE), 2.0)


def draw_keys(key, part):
    return float_portion(key, 202, (SEQUENCE_TOKENS, KEY_VALUE_HEADS * HEAD_SIZE), 1.0)


def draw_values(key, part):
    return float_portion(key, 203, (SEQUENCE_TOKENS, KEY_VALUE_HEADS * HEAD_SIZE), 1.0)


def rope_tables_drawn(position_ids, width):
    half_width = width // 2
    pair_index = jnp.arange(half_width, dtype=jnp.int32)
    first_cut = width // 8
    second_cut = first_cut + 3 * width // 16
    inverse = jnp.exp(pair_index.astype(jnp.float32) * jnp.float32(-2.0 * math.log(THETA) / width))
    picked = jnp.where(pair_index[None, :] < first_cut, position_ids[0][:, None], jnp.where(pair_index[None, :] < second_cut, position_ids[1][:, None], position_ids[2][:, None]))
    angles = picked.astype(jnp.float32) * inverse[None, :]
    cosine_table = jnp.concatenate([jnp.cos(angles), jnp.cos(angles)], axis=-1)
    sine_lookup = jnp.concatenate([jnp.sin(angles), jnp.sin(angles)], axis=-1)
    return (cosine_table, sine_lookup)


def apply_rotation_sampled(field, cosine_table, sine_lookup):
    half_width = field.shape[-1] // 2
    turned = jnp.concatenate([-field[..., half_width:], field[..., :half_width]], axis=-1)
    return field * cosine_table[:, None, :] + turned * sine_lookup[:, None, :]


def forward_pass(key):
    seq_pos, span_ids, span_start = row_info(key)
    allowed = (seq_pos[None, :] <= seq_pos[:, None]) | (span_ids[:, None] == span_ids[None, :]) & (span_ids[:, None] >= 0)
    cosine_table, sine_lookup = rope_tables_drawn(draw_position_ids(key, 0), HEAD_SIZE)
    q_rot = apply_rotation_sampled(draw_queries(key, 0).astype(jnp.float32).reshape(SEQUENCE_TOKENS, QUERY_HEADS, HEAD_SIZE), cosine_table, sine_lookup).astype(jnp.bfloat16)
    rotated_keys = apply_rotation_sampled(draw_keys(key, 0).astype(jnp.float32).reshape(SEQUENCE_TOKENS, KEY_VALUE_HEADS, HEAD_SIZE), cosine_table, sine_lookup).astype(jnp.bfloat16)
    value_heads = draw_values(key, 0).reshape(SEQUENCE_TOKENS, KEY_VALUE_HEADS, HEAD_SIZE)
    score_scale = 1.0 / math.sqrt(HEAD_SIZE)
    query_group_width = QUERY_HEADS // KEY_VALUE_HEADS

    def one_head(head_index):
        kv_index = head_index // query_group_width
        q_head = lax.dynamic_index_in_dim(q_rot, head_index, 1, False)
        k_group = lax.dynamic_index_in_dim(rotated_keys, kv_index, 1, False)
        v_group = lax.dynamic_index_in_dim(value_heads, kv_index, 1, False)
        scores_h = jnp.dot(q_head, k_group.T, preferred_element_type=jnp.float32) * score_scale
        masked = jnp.where(allowed, scores_h, -jnp.inf)
        lse_head = jax.nn.logsumexp(masked, axis=-1)
        probs_h = jnp.exp(masked - lse_head[:, None])
        out_head = jnp.dot(probs_h.astype(jnp.bfloat16), v_group, preferred_element_type=jnp.float32)
        return (lse_head, out_head)
    lse_all, out_all = lax.map(one_head, jnp.arange(QUERY_HEADS, dtype=jnp.int32))
    return (lse_all, out_all.transpose(1, 0, 2).reshape(SEQUENCE_TOKENS, QUERY_HEADS * HEAD_SIZE))


def draw_attn_out(key, part):
    return forward_pass(key)[1].astype(jnp.bfloat16)


def draw_logsumexp(key, part):
    return forward_pass(key)[0].astype(jnp.float32)


def levels(stream_key, dims, shards, least, high):
    gain = 1.0
    for dim, shards_of in shards:
        heights = jax.random.uniform(jax.random.fold_in(jax.random.fold_in(stream_key, 6), dim), (shards_of,), jnp.float32, least / len(shards), high / len(shards))
        gain = gain * jnp.repeat(jnp.exp(heights), dims[dim] // shards_of).reshape((-1,) + (1,) * (len(dims) - 1 - dim))
    return gain


def scatter_about(key, extent, scale, most, cuts=(), kind=jnp.bfloat16):
    array = scale * jax.random.normal(key, extent, jnp.float32)
    if cuts:
        array = array * levels(key, extent, cuts, -0.22, 0.18)
    return jnp.clip(array, -most, most).astype(kind)


def setup_inputs(seed: int = 0) -> dict:
    streams_of = jax.random.split(jax.random.key(seed), 10)
    return {
        "queries": draw_queries(jax.random.fold_in(streams_of[9], 71), 0),
        "keys": draw_keys(jax.random.fold_in(streams_of[9], 71), 0),
        "values": draw_values(jax.random.fold_in(streams_of[9], 71), 0),
        "attn_out": draw_attn_out(jax.random.fold_in(streams_of[9], 71), 0),
        "out_grad": scatter_about(streams_of[4], (SEQUENCE_TOKENS, QUERY_HEADS * HEAD_SIZE), 4.0, 24.0, ((0, 512),)),
        "logsumexp": draw_logsumexp(jax.random.fold_in(streams_of[9], 71), 0),
        "position_ids": draw_position_ids(jax.random.fold_in(streams_of[9], 71), 0),
        "block_map": draw_block_map(jax.random.fold_in(streams_of[9], 71), 0),
        "span_blocks": draw_span_blocks(jax.random.fold_in(streams_of[9], 71), 0),
    }


THETA = 1000000.0

def rope_tables(position_ids, width):
    half_width = width // 2
    pair_index = jnp.arange(half_width, dtype=jnp.int32)
    first_cut = width // 8
    second_cut = first_cut + 3 * width // 16
    inverse = jnp.exp(pair_index.astype(jnp.float32) * jnp.float32(-2.0 * math.log(THETA) / width))
    picked = jnp.where(pair_index[None, :] < first_cut, position_ids[0][:, None], jnp.where(pair_index[None, :] < second_cut, position_ids[1][:, None], position_ids[2][:, None]))
    angles = picked.astype(jnp.float32) * inverse[None, :]
    cosine_table = jnp.concatenate([jnp.cos(angles), jnp.cos(angles)], axis=-1)
    sine_lookup = jnp.concatenate([jnp.sin(angles), jnp.sin(angles)], axis=-1)
    return (cosine_table, sine_lookup)

def apply_rotation(field, cosine_table, sine_lookup):
    half_width = field.shape[-1] // 2
    turned = jnp.concatenate([-field[..., half_width:], field[..., :half_width]], axis=-1)
    return field * cosine_table[:, None, :] + turned * sine_lookup[:, None, :]

def reverse_rotation(field, cosine_table, sine_lookup):
    half_width = field.shape[-1] // 2
    scaled = field * sine_lookup[:, None, :]
    turned = jnp.concatenate([scaled[..., half_width:], -scaled[..., :half_width]], axis=-1)
    return field * cosine_table[:, None, :] + turned

def row_tables(block_map, span_blocks, row_total_count, block_len):
    row_index = jnp.arange(row_total_count, dtype=jnp.int32)
    seq_pos = (jnp.take(block_map, row_index // block_len) * block_len + row_index % block_len).astype(jnp.int32)
    seq_block = seq_pos // block_len
    inside = (seq_block[:, None] >= span_blocks[None, :, 0]) & (seq_block[:, None] < span_blocks[None, :, 1])
    numbers = jnp.arange(span_blocks.shape[0], dtype=jnp.int32)[None, :] + 1
    span_ids = (lax.optimization_barrier(jnp.sum(jnp.where(inside, numbers, 0), axis=1)) - 1).astype(jnp.int32)
    return (seq_pos, span_ids)

def reference(queries, keys, values, attn_out, out_grad, logsumexp, position_ids, block_map, span_blocks):
    row_total_count = queries.shape[0]
    score_scale = 1.0 / math.sqrt(HEAD_SIZE)
    query_group_width = QUERY_HEADS // KEY_VALUE_HEADS
    seq_pos, span_ids = row_tables(block_map, span_blocks, row_total_count, BLK)
    allowed = (seq_pos[None, :] <= seq_pos[:, None]) | (span_ids[:, None] == span_ids[None, :]) & (span_ids[:, None] >= 0)
    cosine_table, sine_lookup = rope_tables(position_ids, HEAD_SIZE)
    q_rot = apply_rotation(queries.astype(jnp.float32).reshape(row_total_count, QUERY_HEADS, HEAD_SIZE), cosine_table, sine_lookup).astype(jnp.bfloat16)
    rotated_keys = apply_rotation(keys.astype(jnp.float32).reshape(row_total_count, KEY_VALUE_HEADS, HEAD_SIZE), cosine_table, sine_lookup).astype(jnp.bfloat16)
    value_heads = values.reshape(row_total_count, KEY_VALUE_HEADS, HEAD_SIZE)
    grad_heads = out_grad.reshape(row_total_count, QUERY_HEADS, HEAD_SIZE)
    delta_rows = lax.optimization_barrier(jnp.sum(out_grad.astype(jnp.float32).reshape(row_total_count, QUERY_HEADS, HEAD_SIZE) * attn_out.astype(jnp.float32).reshape(row_total_count, QUERY_HEADS, HEAD_SIZE), axis=-1))

    def single_key_value(kv_index):
        k_group = lax.dynamic_index_in_dim(rotated_keys, kv_index, 1, False)
        v_group = lax.dynamic_index_in_dim(value_heads, kv_index, 1, False)

        def one_q(loop_state, member):
            head_index = kv_index * query_group_width + member
            q_head = lax.dynamic_index_in_dim(q_rot, head_index, 1, False)
            do_head = lax.dynamic_index_in_dim(grad_heads, head_index, 1, False)
            lse_head = lax.dynamic_index_in_dim(logsumexp, head_index, 0, False)
            delta_head = lax.dynamic_index_in_dim(delta_rows, head_index, 1, False)
            scores_h = jnp.dot(q_head, k_group.T, preferred_element_type=jnp.float32) * score_scale
            probs_h = jnp.exp(jnp.where(allowed, scores_h - lse_head[:, None], -jnp.inf))
            dv_part = jnp.dot(probs_h.astype(jnp.bfloat16).T, do_head, preferred_element_type=jnp.float32)
            grad_p = jnp.dot(do_head, v_group.T, preferred_element_type=jnp.float32)
            grad_s = (probs_h * (grad_p - delta_head[:, None])).astype(jnp.bfloat16)
            dq_head = jnp.dot(grad_s, k_group, preferred_element_type=jnp.float32) * score_scale
            dk_part = jnp.dot(grad_s.T, q_head, preferred_element_type=jnp.float32)
            return ((loop_state[0] + dk_part, loop_state[1] + dv_part), dq_head)
        empty = jnp.zeros((row_total_count, HEAD_SIZE), jnp.float32)
        (dk_group, dv_group), dq_group = lax.scan(one_q, (empty, empty), jnp.arange(query_group_width, dtype=jnp.int32))
        return (dq_group, dk_group * score_scale, dv_group)
    query_gradient_full, key_gradient_full, value_gradient_full = lax.map(single_key_value, jnp.arange(KEY_VALUE_HEADS, dtype=jnp.int32))
    dq_rot = query_gradient_full.reshape(QUERY_HEADS, row_total_count, HEAD_SIZE).transpose(1, 0, 2)
    grad_q = reverse_rotation(dq_rot, cosine_table, sine_lookup).astype(jnp.bfloat16).reshape(row_total_count, QUERY_HEADS * HEAD_SIZE)
    rotated_key_gradient = key_gradient_full.transpose(1, 0, 2)
    key_gradient = reverse_rotation(rotated_key_gradient, cosine_table, sine_lookup).astype(jnp.bfloat16).reshape(row_total_count, KEY_VALUE_HEADS * HEAD_SIZE)
    value_gradient = value_gradient_full.transpose(1, 0, 2).astype(jnp.bfloat16).reshape(row_total_count, KEY_VALUE_HEADS * HEAD_SIZE)
    return (grad_q, key_gradient, value_gradient)
```

```python
import math

import jax
import jax.numpy as jnp
from jax import lax
from jax.experimental import pallas as pl
from jax.experimental.pallas import tpu as pltpu
from jax.sharding import PartitionSpec as P

HEAD = 128
BLK = 64
QUAD = 4
THETA = 1000000.0
LOG2E = 1.4426950408889634
TILE = 256


def rope_tables(position_ids):
    half = HEAD // 2
    pair = jnp.arange(HEAD, dtype=jnp.int32) % half
    inverse = jnp.exp(pair.astype(jnp.float32) * jnp.float32(-2.0 * math.log(THETA) / HEAD))
    first_cut = HEAD // 8
    second_cut = first_cut + 3 * HEAD // 16
    picked = jnp.where(
        pair[None, :] < first_cut,
        position_ids[0][:, None],
        jnp.where(pair[None, :] < second_cut, position_ids[1][:, None], position_ids[2][:, None]),
    )
    angles = picked.astype(jnp.float32) * inverse[None, :]
    sign = jnp.where(jnp.arange(HEAD) < half, -1.0, 1.0).astype(jnp.float32)
    return jnp.cos(angles), jnp.sin(angles) * sign[None, :]


def rotate(field, cosine, sine):
    rows, width = field.shape
    x = field.astype(jnp.float32).reshape(rows, width // HEAD, HEAD)
    out = x * cosine[:, None, :] + jnp.roll(x, HEAD // 2, axis=-1) * sine[:, None, :]
    return out.reshape(rows, width)


def plan(block_map, span_blocks, z, j):
    nz = block_map.shape[0] // (2 * QUAD)
    kseq = lax.dynamic_index_in_dim(block_map.reshape(nz, QUAD, 2), j, 1, False).reshape(-1)
    qseq = lax.dynamic_slice_in_dim(block_map, z * 2 * QUAD, 2 * QUAD)
    rank = jnp.sum(kseq[None, :] < kseq[:, None], axis=1).astype(jnp.int32)
    places = jnp.arange(kseq.shape[0], dtype=jnp.int32)
    hit = rank[None, :] == places[:, None]
    order = jnp.sum(jnp.where(hit, places[None, :], 0), axis=1)
    kseq_sorted = jnp.sum(jnp.where(hit, kseq[None, :], 0), axis=1)
    inside = (qseq[:, None] >= span_blocks[None, :, 0]) & (qseq[:, None] < span_blocks[None, :, 1])
    last = jnp.sum(jnp.where(inside, span_blocks[None, :, 1], 0), axis=1)
    limit = jnp.maximum(qseq, last - 1)
    count = jnp.sum(kseq[None, :] <= limit[:, None], axis=1).astype(jnp.int32)
    per_tile = TILE // BLK
    tiles = (count + per_tile - 1) // per_tile
    return jnp.concatenate([order, kseq_sorted, qseq * BLK, last * BLK - 1, tiles])


def attention_kernel(info, q_ref, do_ref, st_ref, kv_ref, dq_ref, dkv_ref, ks, vs, dk, dv, dqa):
    nk = kv_ref.shape[0] * 2
    nq = q_ref.shape[0] * 2
    heads = q_ref.shape[2] // HEAD
    width = heads * BLK
    scale = 1.0 / math.sqrt(HEAD)
    base = 2 * nk

    def sort(s, carry):
        source = info[s]
        chunk = source // 2
        row = pl.multiple_of((source % 2) * BLK, BLK)
        to = pl.multiple_of(s * BLK, BLK)
        ks[pl.ds(to, BLK), :] = kv_ref[chunk, 0, pl.ds(row, BLK), :]
        vs[pl.ds(to, BLK), :] = kv_ref[chunk, 1, pl.ds(row, BLK), :]
        return carry

    lax.fori_loop(0, nk, sort, 0)
    dk[...] = jnp.zeros_like(dk)
    dv[...] = jnp.zeros_like(dv)
    lane = lax.broadcasted_iota(jnp.int32, (1, width), 1) % BLK
    sub = lax.broadcasted_iota(jnp.int32, (BLK, width), 0)

    def one_block(b, carry):
        m = b // 2
        half = b % 2
        row = pl.multiple_of(half * BLK, BLK)
        q_rows = q_ref[m, pl.ds(row, BLK), :]
        do_rows = do_ref[m, pl.ds(row, BLK), :]
        qb = jnp.concatenate([q_rows[:, h * HEAD : (h + 1) * HEAD] for h in range(heads)], axis=0)
        dob = jnp.concatenate([do_rows[:, h * HEAD : (h + 1) * HEAD] for h in range(heads)], axis=0)
        lse = jnp.concatenate([st_ref[m, 0, half, k : k + 1, :] for k in range(heads // 2)], axis=1)
        delta = jnp.concatenate([st_ref[m, 1, half, k : k + 1, :] for k in range(heads // 2)], axis=1)
        limit = jnp.maximum(info[base + b] + lane, info[base + nq + b])
        dqa[...] = jnp.zeros_like(dqa)

        def one_tile(t, inner):
            at = pl.multiple_of(t * TILE, TILE)
            kt = ks[pl.ds(at, TILE), :]
            vt = vs[pl.ds(at, TILE), :]
            s = lax.dot_general(kt, qb, (((1,), (1,)), ((), ())), preferred_element_type=jnp.float32)
            dp = lax.dot_general(vt, dob, (((1,), (1,)), ((), ())), preferred_element_type=jnp.float32)
            x = s * (scale * LOG2E) - lse
            keep = jnp.concatenate(
                [sub <= limit - info[nk + t * (TILE // BLK) + i] * BLK for i in range(TILE // BLK)], axis=0
            )
            p = jnp.exp2(jnp.where(keep, x, -jnp.inf))
            ds = (p * (dp - delta)).astype(jnp.bfloat16)
            dv[pl.ds(at, TILE), :] += jnp.dot(
                p.astype(jnp.bfloat16), dob, preferred_element_type=jnp.float32
            )
            dk[pl.ds(at, TILE), :] += jnp.dot(ds, qb, preferred_element_type=jnp.float32)
            dqa[...] += lax.dot_general(ds, kt, (((0,), (0,)), ((), ())), preferred_element_type=jnp.float32)
            return inner

        lax.fori_loop(0, info[base + 2 * nq + b], one_tile, 0)
        for h in range(heads):
            dq_ref[m, pl.ds(row, BLK), h * HEAD : (h + 1) * HEAD] = (
                dqa[h * BLK : (h + 1) * BLK, :] * scale
            ).astype(dq_ref.dtype)
        return carry

    lax.fori_loop(0, nq, one_block, 0)

    def unsort(s, carry):
        source = info[s]
        chunk = source // 2
        row = pl.multiple_of((source % 2) * BLK, BLK)
        at = pl.multiple_of(s * BLK, BLK)
        dkv_ref[chunk, 0, pl.ds(row, BLK), :] = (dk[pl.ds(at, BLK), :] * scale).astype(dkv_ref.dtype)
        dkv_ref[chunk, 1, pl.ds(row, BLK), :] = dv[pl.ds(at, BLK), :].astype(dkv_ref.dtype)
        return carry

    lax.fori_loop(0, nk, unsort, 0)


def local_attention(info, q_all, do_all, stats, kv_all):
    chunks, _, rows, _ = kv_all.shape
    columns = chunks * rows
    members, _, width = q_all.shape
    vmem = pl.BlockSpec(memory_space=pltpu.VMEM)
    return pl.pallas_call(
        attention_kernel,
        out_shape=(
            jax.ShapeDtypeStruct((members, rows, width), jnp.bfloat16),
            jax.ShapeDtypeStruct((chunks, 2, rows, HEAD), jnp.bfloat16),
        ),
        in_specs=[pl.BlockSpec(memory_space=pltpu.SMEM), vmem, vmem, vmem, vmem],
        out_specs=(vmem, vmem),
        scratch_shapes=[
            pltpu.VMEM((columns, HEAD), jnp.bfloat16),
            pltpu.VMEM((columns, HEAD), jnp.bfloat16),
            pltpu.VMEM((columns, HEAD), jnp.float32),
            pltpu.VMEM((columns, HEAD), jnp.float32),
            pltpu.VMEM((width // HEAD * BLK, HEAD), jnp.float32),
        ],
        compiler_params=pltpu.CompilerParams(vmem_limit_bytes=40 * 1024 * 1024),
        name="local_attention",
    )(info, q_all, do_all, stats, kv_all)


def by_block(rows_of):
    heads, rows = rows_of.shape
    return rows_of.reshape(heads, 2, BLK).transpose(1, 0, 2).reshape(2, heads // 2, HEAD)


def shards(queries, keys, values, attn_out, out_grad, logsumexp, position_ids, block_map, span_blocks):
    rows, width = queries.shape
    heads = width // HEAD
    shards_of = lax.axis_size("ctx")
    me = lax.axis_index("ctx")
    z, j = me // QUAD, me % QUAD
    quads = [[c * QUAD + i for i in range(QUAD)] for c in range(shards_of // QUAD)]
    lines = [[c * QUAD + i for c in range(shards_of // QUAD)] for i in range(QUAD)]
    info = plan(block_map, span_blocks, z, j)
    cosine, sine = rope_tables(position_ids)
    grad = lax.all_to_all(out_grad, "tp", split_axis=1, concat_axis=0, tiled=True)
    q_rot = rotate(queries, cosine, sine).astype(jnp.bfloat16)
    k_rot = rotate(keys, cosine, sine).astype(jnp.bfloat16)
    delta = jnp.sum(
        (grad.astype(jnp.float32) * attn_out.astype(jnp.float32)).reshape(rows, heads, HEAD), axis=-1
    ).T
    stats = jnp.stack([by_block(logsumexp * LOG2E), by_block(delta)])
    kv = jnp.stack([k_rot, values])
    qd_all = lax.all_gather(jnp.stack([q_rot, grad]), "ctx", axis_index_groups=quads)
    stats_all = lax.all_gather(stats, "ctx", axis_index_groups=quads)
    kv_all = lax.all_gather(kv, "ctx", axis_index_groups=lines)
    dq, dkv = local_attention(info, qd_all[:, 0], qd_all[:, 1], stats_all, kv_all)
    dq = lax.psum_scatter(dq.astype(jnp.float32), "ctx", axis_index_groups=quads)
    dkv = lax.psum_scatter(dkv.astype(jnp.float32), "ctx", axis_index_groups=lines)
    grad_q = rotate(dq, cosine, -sine).astype(jnp.bfloat16)
    key_gradient = rotate(dkv[0], cosine, -sine).astype(jnp.bfloat16)
    return grad_q, key_gradient, dkv[1].astype(jnp.bfloat16)


def solution(mesh):
    return jax.shard_map(
        shards,
        mesh=mesh,
        in_specs=(
            P("ctx", "tp"),
            P("ctx", "tp"),
            P("ctx", "tp"),
            P("ctx", "tp"),
            P(("ctx", "tp"), None),
            P("tp", "ctx"),
            P(None, "ctx"),
            P(),
            P(),
        ),
        out_specs=(P("ctx", "tp"), P("ctx", "tp"), P("ctx", "tp")),
        check_vma=False,
    )
```

```python
import functools
import math

import jax
import jax.numpy as jnp
from jax import lax
from jax.experimental import pallas as pl
from jax.experimental.pallas import tpu as pltpu
from jax.sharding import PartitionSpec as P

HEAD = 128
BLK = 64
QUAD = 4
THETA = 1000000.0
LOG2E = 1.4426950408889634
TILE = 256


def rope_tables(position_ids):
    half = HEAD // 2
    pair = jnp.arange(HEAD, dtype=jnp.int32) % half
    inverse = jnp.exp(pair.astype(jnp.float32) * jnp.float32(-2.0 * math.log(THETA) / HEAD))
    first_cut = HEAD // 8
    second_cut = first_cut + 3 * HEAD // 16
    picked = jnp.where(
        pair[None, :] < first_cut,
        position_ids[0][:, None],
        jnp.where(pair[None, :] < second_cut, position_ids[1][:, None], position_ids[2][:, None]),
    )
    angles = picked.astype(jnp.float32) * inverse[None, :]
    sign = jnp.where(jnp.arange(HEAD) < half, -1.0, 1.0).astype(jnp.float32)
    return jnp.cos(angles), jnp.sin(angles) * sign[None, :]


def plan(block_map, span_blocks, z, j):
    nz = block_map.shape[0] // (2 * QUAD)
    kseq = lax.dynamic_index_in_dim(block_map.reshape(nz, QUAD, 2), j, 1, False).reshape(-1)
    qseq = lax.dynamic_slice_in_dim(block_map, z * 2 * QUAD, 2 * QUAD)
    rank = jnp.sum(kseq[None, :] < kseq[:, None], axis=1).astype(jnp.int32)
    places = jnp.arange(kseq.shape[0], dtype=jnp.int32)
    hit = rank[None, :] == places[:, None]
    order = jnp.sum(jnp.where(hit, places[None, :], 0), axis=1)
    kseq_sorted = jnp.sum(jnp.where(hit, kseq[None, :], 0), axis=1)
    inside = (qseq[:, None] >= span_blocks[None, :, 0]) & (qseq[:, None] < span_blocks[None, :, 1])
    last = jnp.sum(jnp.where(inside, span_blocks[None, :, 1], 0), axis=1)
    limit = jnp.maximum(qseq, last - 1)
    count = jnp.sum(kseq[None, :] <= limit[:, None], axis=1).astype(jnp.int32)
    per_tile = TILE // BLK
    tiles = (count + per_tile - 1) // per_tile
    return jnp.concatenate([order, kseq_sorted, qseq * BLK, last * BLK - 1, tiles])


def attention_kernel(info, q_ref, do_ref, st_ref, kv_ref, dq_ref, dkv_ref, ks, vs, dk, dv, dqa):
    nk = kv_ref.shape[0] * 2
    nq = q_ref.shape[0] * 2
    heads = q_ref.shape[2] // HEAD
    width = heads * BLK
    scale = 1.0 / math.sqrt(HEAD)
    base = 2 * nk

    def sort(s, carry):
        source = info[s]
        chunk = source // 2
        row = pl.multiple_of((source % 2) * BLK, BLK)
        to = pl.multiple_of(s * BLK, BLK)
        ks[pl.ds(to, BLK), :] = kv_ref[chunk, 0, pl.ds(row, BLK), :]
        vs[pl.ds(to, BLK), :] = kv_ref[chunk, 1, pl.ds(row, BLK), :]
        return carry

    lax.fori_loop(0, nk, sort, 0)
    dk[...] = jnp.zeros_like(dk)
    dv[...] = jnp.zeros_like(dv)
    lane = lax.broadcasted_iota(jnp.int32, (1, width), 1) % BLK
    sub = lax.broadcasted_iota(jnp.int32, (BLK, width), 0)

    def one_block(b, carry):
        m = b // 2
        half = b % 2
        row = pl.multiple_of(half * BLK, BLK)
        q_rows = q_ref[m, pl.ds(row, BLK), :]
        do_rows = do_ref[m, pl.ds(row, BLK), :]
        qb = jnp.concatenate([q_rows[:, h * HEAD : (h + 1) * HEAD] for h in range(heads)], axis=0)
        dob = jnp.concatenate([do_rows[:, h * HEAD : (h + 1) * HEAD] for h in range(heads)], axis=0)
        lse = jnp.concatenate([st_ref[m, 0, half, k : k + 1, :] for k in range(heads // 2)], axis=1)
        delta = jnp.concatenate([st_ref[m, 1, half, k : k + 1, :] for k in range(heads // 2)], axis=1)
        limit = jnp.maximum(info[base + b] + lane, info[base + nq + b])
        dqa[...] = jnp.zeros_like(dqa)

        def one_tile(t, inner):
            at = pl.multiple_of(t * TILE, TILE)
            kt = ks[pl.ds(at, TILE), :]
            vt = vs[pl.ds(at, TILE), :]
            s = lax.dot_general(kt, qb, (((1,), (1,)), ((), ())), preferred_element_type=jnp.float32)
            dp = lax.dot_general(vt, dob, (((1,), (1,)), ((), ())), preferred_element_type=jnp.float32)
            x = s * (scale * LOG2E) - lse
            keep = jnp.concatenate(
                [sub <= limit - info[nk + t * (TILE // BLK) + i] * BLK for i in range(TILE // BLK)], axis=0
            )
            p = jnp.exp2(jnp.where(keep, x, -jnp.inf))
            ds = (p * (dp - delta)).astype(jnp.bfloat16)
            dv[pl.ds(at, TILE), :] += jnp.dot(
                p.astype(jnp.bfloat16), dob, preferred_element_type=jnp.float32
            )
            dk[pl.ds(at, TILE), :] += jnp.dot(ds, qb, preferred_element_type=jnp.float32)
            dqa[...] += lax.dot_general(ds, kt, (((0,), (0,)), ((), ())), preferred_element_type=jnp.float32)
            return inner

        lax.fori_loop(0, info[base + 2 * nq + b], one_tile, 0)
        for h in range(heads):
            dq_ref[m, pl.ds(row, BLK), h * HEAD : (h + 1) * HEAD] = (
                dqa[h * BLK : (h + 1) * BLK, :] * scale
            ).astype(dq_ref.dtype)
        return carry

    lax.fori_loop(0, nq, one_block, 0)

    def unsort(s, carry):
        source = info[s]
        chunk = source // 2
        row = pl.multiple_of((source % 2) * BLK, BLK)
        at = pl.multiple_of(s * BLK, BLK)
        dkv_ref[chunk, 0, pl.ds(row, BLK), :] = (dk[pl.ds(at, BLK), :] * scale).astype(dkv_ref.dtype)
        dkv_ref[chunk, 1, pl.ds(row, BLK), :] = dv[pl.ds(at, BLK), :].astype(dkv_ref.dtype)
        return carry

    lax.fori_loop(0, nk, unsort, 0)


def local_attention(info, q_all, do_all, stats, kv_all):
    chunks, _, rows, _ = kv_all.shape
    columns = chunks * rows
    members, _, width = q_all.shape
    vmem = pl.BlockSpec(memory_space=pltpu.VMEM)
    return pl.pallas_call(
        attention_kernel,
        out_shape=(
            jax.ShapeDtypeStruct((members, rows, width), jnp.bfloat16),
            jax.ShapeDtypeStruct((chunks, 2, rows, HEAD), jnp.bfloat16),
        ),
        in_specs=[pl.BlockSpec(memory_space=pltpu.SMEM), vmem, vmem, vmem, vmem],
        out_specs=(vmem, vmem),
        scratch_shapes=[
            pltpu.VMEM((columns, HEAD), jnp.bfloat16),
            pltpu.VMEM((columns, HEAD), jnp.bfloat16),
            pltpu.VMEM((columns, HEAD), jnp.float32),
            pltpu.VMEM((columns, HEAD), jnp.float32),
            pltpu.VMEM((width // HEAD * BLK, HEAD), jnp.float32),
        ],
        compiler_params=pltpu.CompilerParams(vmem_limit_bytes=40 * 1024 * 1024),
        name="local_attention",
    )(info, q_all, do_all, stats, kv_all)


MESH = pl.DeviceIdType.MESH


def places(heads_axis):
    me = lax.axis_index("ctx")
    z, j = me // QUAD, me % QUAD
    yh, core = j // 2, j % 2
    return me, z, j, yh, core, lax.axis_index(heads_axis)


def signal_all(barrier, peers):
    for peer in peers:
        pl.semaphore_signal(barrier, inc=1, device_id=peer, device_id_type=MESH)
    pl.semaphore_wait(barrier, len(peers))


def send(source, target, send_sem, recv_sem, peer):
    return pltpu.make_async_remote_copy(
        src_ref=source,
        dst_ref=target,
        send_sem=send_sem,
        recv_sem=recv_sem,
        device_id=peer,
        device_id_type=MESH,
    )


def gather_kernel(
    nz, ntp, q_in, k_in, v_in, out_in, grad_in, lse_in, cos_in, sin_in,
    q_all, do_all, stats, kv_all,
    do_send, do_recv, own_sem, ring_send, ring_recv, q_send, q_recv, fwd_send, fwd_recv, st_send, st_recv,
):
    me, z, j, yh, core, tp = places("tp")
    rows, width = q_in.shape
    heads = width // HEAD
    slab = rows // ntp
    n = nz * QUAD
    right = {"ctx": (me + QUAD) % n, "tp": tp}
    left = {"ctx": (me + n - QUAD) % n, "tp": tp}
    to_core = me + 1 - 2 * core
    to_y = me + 2 - 4 * yh
    diagonal = to_core + 2 - 4 * yh
    core_peer = {"ctx": to_core, "tp": tp}
    y_peer = {"ctx": to_y, "tp": tp}
    far_peer = {"ctx": diagonal, "tp": tp}
    j_y = j + 2 - 4 * yh
    others = [{"ctx": where, "tp": (tp + i) % ntp} for where in (me, to_y) for i in range(1, ntp)]
    signal_all(pltpu.get_barrier_semaphore(), [right, left, core_peer, y_peer, far_peer, *others])

    mine = pl.ds(pl.multiple_of(tp * slab, slab), slab)
    copies = []
    own = None
    for i in range(ntp):
        t = (tp + i) % ntp
        part = grad_in.at[:, pl.ds(pl.multiple_of(t * width, width), width)]
        for a, where in enumerate((me, to_y)):
            if i == 0 and a == 0:
                own = pltpu.make_async_copy(part, do_all.at[j, mine, :], own_sem)
                own.start()
            else:
                copies.append(
                    send(part, do_all.at[j, mine, :], do_send.at[a, i], do_recv.at[a, i], {"ctx": where, "tp": t})
                )
                copies[-1].start()

    cosine, sine = cos_in[...], sin_in[...]
    k = k_in[...].astype(jnp.float32)
    kv_all[z, 0] = (k * cosine + pltpu.roll(k, HEAD // 2, 1) * sine).astype(jnp.bfloat16)
    kv_all[z, 1] = v_in[...]
    hops = (nz // 2, nz // 2 - 1)

    def hop(d, s, piece):
        slot = (z - s + nz) % nz if d == 0 else (z + s) % nz
        ref = kv_all.at[slot, piece]
        return send(ref, ref, ring_send.at[d, s, piece], ring_recv.at[d, s, piece], right if d == 0 else left)

    def arrived(d, s, piece):
        slot = (z - s - 1 + nz) % nz if d == 0 else (z + s + 1) % nz
        ref = kv_all.at[slot, piece]
        return send(ref, ref, ring_send.at[d, s, piece], ring_recv.at[d, s, piece], right if d == 0 else left)

    for piece in range(2):
        for d in range(2):
            if hops[d] > 0:
                hop(d, 0, piece).start()

    for h in range(heads):
        at = slice(h * HEAD, (h + 1) * HEAD)
        x = q_in[:, at].astype(jnp.float32)
        q_all[j, :, at] = (x * cosine + pltpu.roll(x, HEAD // 2, 1) * sine).astype(jnp.bfloat16)
    q_y = send(q_all.at[j], q_all.at[j], q_send.at[0], q_recv.at[0], y_peer)
    q_core = send(q_all.at[j], q_all.at[j], q_send.at[1], q_recv.at[1], core_peer)
    q_y.start()
    q_core.start()

    def steps(first, last):
        def one(s, carry):
            for piece in range(2):
                for d in range(2):
                    arrived(d, s - 1, piece).wait_recv()
                    hop(d, s, piece).start()
            return carry

        lax.fori_loop(first, last, one, 0)

    middle = (1 + hops[1]) // 2
    steps(1, middle)

    own.wait()
    for i in range(1, ntp):
        t = (tp - i + ntp) % ntp
        there = do_all.at[j, pl.ds(pl.multiple_of(t * slab, slab), slab), :]
        send(there, there, do_send.at[0, i], do_recv.at[0, i], core_peer).wait_recv()
    forward = [send(do_all.at[j], do_all.at[j], fwd_send.at[0], fwd_recv.at[0], core_peer)]
    forward[0].start()
    lane = lax.broadcasted_iota(jnp.int32, (1, HEAD), 1)
    for k2 in range(heads // 2):
        pair = []
        for h in (2 * k2, 2 * k2 + 1):
            at = slice(h * HEAD, (h + 1) * HEAD)
            product = do_all[j, :, at].astype(jnp.float32) * out_in[:, at].astype(jnp.float32)
            pair.append((lse_in[h : h + 1, :] * LOG2E, jnp.sum(product.T, axis=0, keepdims=True)))
        for what in range(2):
            a, b = pair[0][what], pair[1][what]
            stats[j, what, 0, k2 : k2 + 1, :] = jnp.where(lane < BLK, a, pltpu.roll(b, BLK, 1))
            stats[j, what, 1, k2 : k2 + 1, :] = jnp.where(lane < BLK, pltpu.roll(a, BLK, 1), b)
    small = [
        send(stats.at[j], stats.at[j], st_send.at[i], st_recv.at[i], peer)
        for i, peer in enumerate((core_peer, y_peer, far_peer))
    ]
    for copy in small:
        copy.start()

    send(q_all.at[j_y], q_all.at[j_y], q_send.at[0], q_recv.at[0], y_peer).wait_recv()
    forward.append(send(q_all.at[j_y], q_all.at[j_y], fwd_send.at[1], fwd_recv.at[1], core_peer))
    forward[1].start()
    steps(middle, hops[1])
    for i in range(ntp):
        t = (tp - i + ntp) % ntp
        there = do_all.at[j_y, pl.ds(pl.multiple_of(t * slab, slab), slab), :]
        send(there, there, do_send.at[1, i], do_recv.at[1, i], core_peer).wait_recv()
    forward.append(send(do_all.at[j_y], do_all.at[j_y], fwd_send.at[2], fwd_recv.at[2], core_peer))
    forward[2].start()

    for piece in range(2):
        if hops[1] > 0:
            arrived(0, hops[1] - 1, piece).wait_recv()
            hop(0, hops[1], piece).start()
            arrived(1, hops[1] - 1, piece).wait_recv()
    for piece in range(2):
        arrived(0, hops[0] - 1, piece).wait_recv()
    for d in range(2):
        for s in range(hops[d]):
            for piece in range(2):
                hop(d, s, piece).wait_send()
    for copy in copies:
        copy.wait_send()
    q_y.wait_send()
    q_core.wait()
    for copy in forward:
        copy.wait()
    for copy in small:
        copy.wait()


def gather(queries, keys, values, attn_out, out_grad, logsumexp, cosine, sine):
    rows, width = queries.shape
    heads = width // HEAD
    nz = lax.axis_size("ctx") // QUAD
    ntp = lax.axis_size("tp")
    vmem = pl.BlockSpec(memory_space=pltpu.VMEM)
    dma = pltpu.SemaphoreType.DMA
    return pl.pallas_call(
        functools.partial(gather_kernel, nz, ntp),
        out_shape=(
            jax.ShapeDtypeStruct((QUAD, rows, width), jnp.bfloat16),
            jax.ShapeDtypeStruct((QUAD, rows, width), jnp.bfloat16),
            jax.ShapeDtypeStruct((QUAD, 2, 2, heads // 2, HEAD), jnp.float32),
            jax.ShapeDtypeStruct((nz, 2, rows, HEAD), jnp.bfloat16),
        ),
        in_specs=[vmem, vmem, vmem, vmem, pl.BlockSpec(memory_space=pl.ANY), vmem, vmem, vmem],
        out_specs=(vmem, vmem, vmem, vmem),
        scratch_shapes=[
            dma((2, ntp)), dma((2, ntp)), dma, dma((2, nz // 2, 2)), dma((2, nz // 2, 2)),
            dma((2,)), dma((2,)), dma((3,)), dma((3,)), dma((3,)), dma((3,)),
        ],
        compiler_params=pltpu.CompilerParams(
            vmem_limit_bytes=40 * 1024 * 1024, collective_id=0, has_side_effects=True
        ),
        name="gather_inputs",
    )(queries, keys, values, attn_out, out_grad, logsumexp, cosine, sine)


def reduce_kernel(
    nz, dq_in, dkv_in, cos_in, sin_in, gq_out, gk_out, gv_out,
    ring, first, second, total, ring_send, ring_recv, core_send, core_recv, y_send, y_recv,
):
    me, z, j, yh, core, tp = places("tp")
    rows, width = gq_out.shape
    heads = width // HEAD
    n = nz * QUAD
    right = {"ctx": (me + QUAD) % n, "tp": tp}
    left = {"ctx": (me + n - QUAD) % n, "tp": tp}
    core_peer = {"ctx": me + 1 - 2 * core, "tp": tp}
    y_peer = {"ctx": me + 2 - 4 * yh, "tp": tp}
    signal_all(pltpu.get_barrier_semaphore(), [right, left, core_peer, y_peer])
    hops = (nz // 2, nz // 2 - 1)

    def owner(d, s):
        return (z + hops[0] - s) % nz if d == 0 else (z - hops[1] + s + nz) % nz

    def hop(d, s, piece, source):
        return send(
            source, ring.at[d, s, piece], ring_send.at[d, s, piece], ring_recv.at[d, s, piece],
            right if d == 0 else left,
        )

    for piece in range(2):
        for d in range(2):
            if hops[d] > 0:
                hop(d, 0, piece, dkv_in.at[owner(d, 0), piece]).start()
    wanted = [2 * (1 - yh) + core, j]
    to_core = [
        send(dq_in.at[m + 1 - 2 * core], first.at[i], core_send.at[i], core_recv.at[i], core_peer)
        for i, m in enumerate(wanted)
    ]
    for copy in to_core:
        copy.start()
    to_core[0].wait_recv()
    total[...] = (dq_in[wanted[0]].astype(jnp.float32) + first[0].astype(jnp.float32)).astype(jnp.bfloat16)
    to_y = send(total, second, y_send, y_recv, y_peer)
    to_y.start()

    def step(d, s, piece):
        hop(d, s - 1, piece, ring.at[d, s - 1, piece]).wait_recv()
        ring[d, s - 1, piece] = (
            ring[d, s - 1, piece].astype(jnp.float32) + dkv_in[owner(d, s), piece].astype(jnp.float32)
        ).astype(jnp.bfloat16)
        hop(d, s, piece, ring.at[d, s - 1, piece]).start()

    def steps(s, carry):
        for piece in range(2):
            for d in range(2):
                step(d, s, piece)
        return carry

    lax.fori_loop(1, hops[1], steps, 0)
    if hops[1] > 0:
        for piece in range(2):
            step(0, hops[1], piece)
    to_core[1].wait_recv()
    to_y.wait_recv()
    cosine, sine = cos_in[...], sin_in[...]
    for h in range(heads):
        at = slice(h * HEAD, (h + 1) * HEAD)
        x = (
            dq_in[j, :, at].astype(jnp.float32)
            + first[1, :, at].astype(jnp.float32)
            + second[:, at].astype(jnp.float32)
        )
        gq_out[:, at] = (x * cosine - pltpu.roll(x, HEAD // 2, 1) * sine).astype(jnp.bfloat16)
    for piece in range(2):
        x = dkv_in[z, piece].astype(jnp.float32)
        for d in range(2):
            if hops[d] > 0:
                last = ring.at[d, hops[d] - 1, piece]
                hop(d, hops[d] - 1, piece, last).wait_recv()
                x = x + last[...].astype(jnp.float32)
        if piece == 0:
            gk_out[...] = (x * cosine - pltpu.roll(x, HEAD // 2, 1) * sine).astype(jnp.bfloat16)
        else:
            gv_out[...] = x.astype(jnp.bfloat16)
    for d in range(2):
        for s in range(hops[d]):
            for piece in range(2):
                hop(d, s, piece, ring.at[d, s, piece]).wait_send()
    for copy in (*to_core, to_y):
        copy.wait_send()


def scatter(dq, dkv, cosine, sine):
    nz, _, rows, _ = dkv.shape
    width = dq.shape[2]
    vmem = pl.BlockSpec(memory_space=pltpu.VMEM)
    dma = pltpu.SemaphoreType.DMA
    return pl.pallas_call(
        functools.partial(reduce_kernel, nz),
        out_shape=(
            jax.ShapeDtypeStruct((rows, width), jnp.bfloat16),
            jax.ShapeDtypeStruct((rows, HEAD), jnp.bfloat16),
            jax.ShapeDtypeStruct((rows, HEAD), jnp.bfloat16),
        ),
        in_specs=[vmem] * 4,
        out_specs=(vmem, vmem, vmem),
        scratch_shapes=[
            pltpu.VMEM((2, nz // 2, 2, rows, HEAD), jnp.bfloat16),
            pltpu.VMEM((2, rows, width), jnp.bfloat16),
            pltpu.VMEM((rows, width), jnp.bfloat16),
            pltpu.VMEM((rows, width), jnp.bfloat16),
            dma((2, nz // 2, 2)), dma((2, nz // 2, 2)), dma((2,)), dma((2,)), dma, dma,
        ],
        compiler_params=pltpu.CompilerParams(
            vmem_limit_bytes=40 * 1024 * 1024, collective_id=1, has_side_effects=True
        ),
        name="scatter_gradients",
    )(dq, dkv, cosine, sine)


def shards(queries, keys, values, attn_out, out_grad, logsumexp, position_ids, block_map, span_blocks):
    me = lax.axis_index("ctx")
    info = plan(block_map, span_blocks, me // QUAD, me % QUAD)
    cosine, sine = rope_tables(position_ids)
    q_all, do_all, stats, kv_all = gather(
        queries, keys, values, attn_out, out_grad, logsumexp, cosine, sine
    )
    dq, dkv = local_attention(info, q_all, do_all, stats, kv_all)
    return scatter(dq, dkv, cosine, sine)


def solution(mesh):
    return jax.shard_map(
        shards,
        mesh=mesh,
        in_specs=(
            P("ctx", "tp"),
            P("ctx", "tp"),
            P("ctx", "tp"),
            P("ctx", "tp"),
            P(("ctx", "tp"), None),
            P("tp", "ctx"),
            P(None, "ctx"),
            P(),
            P(),
        ),
        out_specs=(P("ctx", "tp"), P("ctx", "tp"), P("ctx", "tp")),
        check_vma=False,
    )
```

```python
import functools
import math

import jax
import jax.numpy as jnp
from jax import lax
from jax.experimental import pallas as pl
from jax.experimental.pallas import tpu as pltpu
from jax.sharding import PartitionSpec as P

HEAD = 128
BLK = 64
QUAD = 4
THETA = 1000000.0
LOG2E = 1.4426950408889634


def rope_tables(position_ids):
    half = HEAD // 2
    pair = jnp.arange(HEAD, dtype=jnp.int32) % half
    inverse = jnp.exp(pair.astype(jnp.float32) * jnp.float32(-2.0 * math.log(THETA) / HEAD))
    first_cut = HEAD // 8
    second_cut = first_cut + 3 * HEAD // 16
    picked = jnp.where(
        pair[None, :] < first_cut,
        position_ids[0][:, None],
        jnp.where(pair[None, :] < second_cut, position_ids[1][:, None], position_ids[2][:, None]),
    )
    angles = picked.astype(jnp.float32) * inverse[None, :]
    sign = jnp.where(jnp.arange(HEAD) < half, -1.0, 1.0).astype(jnp.float32)
    return jnp.cos(angles), jnp.sin(angles) * sign[None, :]


MESH = pl.DeviceIdType.MESH


def signal_all(barrier, peers):
    for peer in peers:
        pl.semaphore_signal(barrier, inc=1, device_id=peer, device_id_type=MESH)
    pl.semaphore_wait(barrier, len(peers))


def send(source, target, send_sem, recv_sem, peer):
    return pltpu.make_async_remote_copy(
        src_ref=source,
        dst_ref=target,
        send_sem=send_sem,
        recv_sem=recv_sem,
        device_id=peer,
        device_id_type=MESH,
    )


def step_kernel(
    nz, ntp, map_in, span_in, q_in, k_in, v_in, out_in, grad_in, lse_in, cos_in, sin_in,
    gq_out, gk_out, gv_out,
    q_raw, out_raw, lse_raw, k_raw, q_all, do_all, stats, kv, part, dq, dq_go, first, second, carry, stage, back, limits,
    local, do_send, do_recv, kv_send, kv_recv, q_send, q_recv, fwd_send, fwd_recv, st_send, st_recv,
    rs_send, rs_recv, dq_send, dq_recv,
):
    me = lax.axis_index("ctx")
    tp = lax.axis_index("tp")
    z, j = me // QUAD, me % QUAD
    yh, core = j // 2, j % 2
    rows, width = gq_out.shape
    heads = width // HEAD
    slab = rows // ntp
    n = nz * QUAD
    half = nz // 2
    far = (half, half - 1)
    scale = 1.0 / math.sqrt(HEAD)
    at_core = me + 1 - 2 * core
    at_y = me + 2 - 4 * yh
    core_peer = {"ctx": at_core, "tp": tp}
    y_peer = {"ctx": at_y, "tp": tp}
    cross_peer = {"ctx": at_core + 2 - 4 * yh, "tp": tp}
    along = {k: {"ctx": (me + QUAD * k + n) % n, "tp": tp} for k in (1, 2, -1, -2)}

    loads = [
        pltpu.make_async_copy(source, target, local.at[i])
        for i, (source, target) in enumerate(
            ((k_in, k_raw), (v_in, kv.at[0, 1, pl.ds(rows, rows), :]), (q_in, q_raw), (out_in, out_raw), (lse_in, lse_raw))
        )
    ]
    for load in loads:
        load.start()
    others = [{"ctx": where, "tp": (tp + i) % ntp} for where in (me, at_y) for i in range(1, ntp)]
    signal_all(
        pltpu.get_barrier_semaphore(), [*along.values(), core_peer, y_peer, cross_peer, *others]
    )

    def shard(d, a):
        if a == 0 or a == half:
            return kv.at[0, :, pl.ds(rows if a == 0 else 0, rows), :]
        return kv.at[a, :, pl.ds(rows if d == 0 else 0, rows), :]

    def pass_on(d, a, from_a, places):
        return send(
            shard(d, from_a), shard(d, a), kv_send.at[d, a], kv_recv.at[d, a], along[places if d == 0 else -places]
        )

    def arrived(a):
        for d in range(2):
            if a <= far[d]:
                pass_on(d, a, a, 1).wait_recv()
            if a + 2 <= far[d]:
                pass_on(d, a + 2, a, 2).start()

    cosine, sine = cos_in[...], sin_in[...]
    loads[0].wait()
    loads[1].wait()
    k = k_raw[...].astype(jnp.float32)
    kv[0, 0, rows : 2 * rows, :] = (k * cosine + pltpu.roll(k, HEAD // 2, 1) * sine).astype(jnp.bfloat16)
    for a in (2, 1):
        for d in range(2):
            if a <= far[d]:
                pass_on(d, a, 0, a).start()

    mine = pl.ds(pl.multiple_of(tp * slab, slab), slab)
    copies = []
    own = None
    for i in range(ntp):
        t = (tp + i) % ntp
        piece = grad_in.at[:, pl.ds(pl.multiple_of(t * width, width), width)]
        for a, where in enumerate((me, at_y)):
            if i == 0 and a == 0:
                own = pltpu.make_async_copy(piece, do_all.at[2, mine, :], local.at[5])
                own.start()
            else:
                slot = 2 if a == 0 else 0
                copies.append(
                    send(piece, do_all.at[slot, mine, :], do_send.at[a, i], do_recv.at[a, i], {"ctx": where, "tp": t})
                )
                copies[-1].start()

    loads[2].wait()
    for h in range(heads):
        at = slice(h * HEAD, (h + 1) * HEAD)
        x = q_raw[:, at].astype(jnp.float32)
        q_all[2, at, :] = (x * cosine + pltpu.roll(x, HEAD // 2, 1) * sine).astype(jnp.bfloat16)
    q_y = send(q_all.at[2], q_all.at[0], q_send.at[0], q_recv.at[0], y_peer)
    q_core = send(q_all.at[2], q_all.at[3], q_send.at[1], q_recv.at[1], core_peer)
    q_y.start()
    q_core.start()

    arrived(1)
    lane = lax.broadcasted_iota(jnp.int32, (1, HEAD), 1)
    dq[...] = jnp.zeros_like(dq)

    def limit_of(block):
        place = map_in[block]
        end = jnp.int32(0)
        for i in range(span_in.shape[0]):
            inside = (place >= span_in[i, 0]) & (place < span_in[i, 1])
            end = end + jnp.where(inside, span_in[i, 1], 0)
        return place * BLK, end * BLK - 1

    for slot, member in enumerate((j + 2 - 4 * yh, (j + 2 - 4 * yh) + 1 - 2 * core, j, j + 1 - 2 * core)):
        pieces = []
        for b in range(2):
            place, end = limit_of((z * QUAD + member) * 2 + b)
            pieces.append(jnp.maximum(place + lane - b * BLK, end))
        limits[slot : slot + 1, :] = jnp.where(lane < BLK, pieces[0], pieces[1])
    for a in range(2, min(4, half - 1)):
        arrived(a)

    def from_slot(slot, axis, i):
        t = (tp - i + ntp) % ntp
        there = do_all.at[slot, pl.ds(pl.multiple_of(t * slab, slab), slab), :]
        return send(there, there, do_send.at[axis, i], do_recv.at[axis, i], core_peer)

    own.wait()
    for i in range(1, ntp):
        from_slot(2, 0, i).wait_recv()
    forward = [send(do_all.at[2], do_all.at[3], fwd_send.at[0], fwd_recv.at[0], core_peer)]
    forward[0].start()
    loads[3].wait()
    loads[4].wait()
    for h in range(heads):
        at = slice(h * HEAD, (h + 1) * HEAD)
        product = do_all[2, :, at].astype(jnp.float32) * out_raw[:, at].astype(jnp.float32)
        stats[2, 0, h : h + 1, :] = lse_raw[h : h + 1, :] * LOG2E
        stats[2, 1, h : h + 1, :] = jnp.sum(product.T, axis=0, keepdims=True)
    small = [
        send(stats.at[2], stats.at[slot], st_send.at[i], st_recv.at[i], peer)
        for i, (slot, peer) in enumerate(((3, core_peer), (0, y_peer), (1, cross_peer)))
    ]
    for copy in small:
        copy.start()
    q_y.wait_recv()
    forward.append(send(q_all.at[0], q_all.at[1], fwd_send.at[1], fwd_recv.at[1], core_peer))
    forward[1].start()
    for a in range(4, half - 1):
        arrived(a)
    for i in range(ntp):
        from_slot(0, 1, i).wait_recv()
    forward.append(send(do_all.at[0], do_all.at[1], fwd_send.at[2], fwd_recv.at[2], core_peer))
    forward[2].start()
    for copy in (q_core, *forward, *small):
        copy.wait_recv()

    sub = lax.broadcasted_iota(jnp.int32, (BLK, HEAD), 0)

    def unit(p, g, keep_part):
        kp, vp = kv[p, 0], kv[p, 1]
        slots = (2 * g, 2 * g + 1)
        qs = jnp.concatenate([q_all[slot] for slot in slots], axis=0)
        grads = jnp.concatenate(
            [do_all[slot, :, h * HEAD : (h + 1) * HEAD] for slot in slots for h in range(heads)], axis=0
        )
        up = (p + half - 1) % half + 1
        shards_z = ((z + up) % nz, (z - p + nz) % nz)
        places = [map_in[(s * QUAD + j) * 2 + b] * BLK for s in shards_z for b in range(2)]
        s = lax.dot_general(kp, qs, (((1,), (1,)), ((), ())), preferred_element_type=jnp.float32)
        dp = lax.dot_general(vp, grads, (((1,), (1,)), ((), ())), preferred_element_type=jnp.float32)
        probs, scores = [], []
        for i, slot in enumerate(slots):
            bound = limits[slot : slot + 1, :]
            allowed = jnp.concatenate([sub <= bound - place for place in places], axis=0)
            for h in range(heads):
                at = slice((i * heads + h) * HEAD, (i * heads + h + 1) * HEAD)
                x = s[:, at] * (scale * LOG2E) - stats[slot, 0, h : h + 1, :]
                prob = jnp.exp2(jnp.where(allowed, x, -jnp.inf))
                probs.append(prob.astype(jnp.bfloat16))
                scores.append((prob * (dp[:, at] - stats[slot, 1, h : h + 1, :])).astype(jnp.bfloat16))
        probs = jnp.concatenate(probs, axis=1)
        scores = jnp.concatenate(scores, axis=1)
        dv = jnp.dot(probs, grads, preferred_element_type=jnp.float32)
        dk = jnp.dot(scores, qs, preferred_element_type=jnp.float32) * scale
        if keep_part:
            part[p, 0] += dk
            part[p, 1] += dv
        else:
            part[p, 0] = dk
            part[p, 1] = dv
        dq[g] += lax.dot_general(scores, kp, (((0,), (0,)), ((), ())), preferred_element_type=jnp.float32)

    def part_of(d, s, p):
        return part[p, :, (0 if d == 0 else rows) : (rows if d == 0 else 2 * rows), :]

    def give(d, s, source, places):
        return send(
            source, carry.at[d, s], rs_send.at[d, s], rs_recv.at[d, s], along[places if d == 0 else -places]
        )

    def start_chain(d, s, p, places):
        at = far[d] - s
        stage[d, at] = part_of(d, s, p).astype(jnp.bfloat16)
        give(d, s, stage.at[d, at], places).start()

    def add_and_give(d, s, p, places):
        give(d, s + 2, carry.at[d, s + 2], 1).wait_recv()
        carry[d, s + 2] = (carry[d, s + 2].astype(jnp.float32) + part_of(d, s, p)).astype(jnp.bfloat16)
        give(d, s, carry.at[d, s + 2], places).start()

    to_core = [send(dq_go.at[i], first.at[i], dq_send.at[i], dq_recv.at[i], core_peer) for i in range(2)]
    span_rows = heads * HEAD

    def one_pair(i, unused):
        p = (half + 1 - i) % half
        s = half + 1 - i

        @pl.when(i == 1)
        def _():
            pass_on(0, half, half, 1).wait_recv()

        if half - 1 > 1:

            @pl.when(i == 2)
            def _():
                arrived(half - 1)

        unit(p, 0, False)

        @pl.when(i == half - 1)
        def _():
            dq_go[0] = (dq[0, span_rows : 2 * span_rows, :] * scale).astype(jnp.bfloat16)
            to_core[0].start()

        unit(p, 1, True)
        for d in range(2):

            @pl.when((i >= 1 + d) & (i <= 2 + d))
            def _():
                start_chain(d, s, p, 2)

            if half > 3 + d:

                @pl.when(i >= 3 + d)
                def _():
                    add_and_give(d, s, p, 2)

        return unused

    lax.fori_loop(0, half, one_pair, 0)
    dq_go[1] = (dq[1, span_rows : 2 * span_rows, :] * scale).astype(jnp.bfloat16)
    to_core[1].start()
    for d in range(2):
        if far[d] >= 3:
            add_and_give(d, 1, 1, 1)
        else:
            start_chain(d, 1, 1, 1)
    to_core[0].wait_recv()
    back[...] = (dq[0, 0:span_rows, :] * scale + first[0].astype(jnp.float32)).astype(jnp.bfloat16)
    to_y = send(back, second, dq_send.at[2], dq_recv.at[2], y_peer)
    to_y.start()
    to_core[1].wait_recv()
    ends = [part[0, what, rows : 2 * rows, :] for what in range(2)]
    for d in range(2):
        for s in (2, 1):
            if s <= far[d]:
                give(d, s, carry.at[d, s], 1).wait_recv()
                ends = [ends[what] + carry[d, s, what].astype(jnp.float32) for what in range(2)]
    gk_out[...] = (ends[0] * cosine - pltpu.roll(ends[0], HEAD // 2, 1) * sine).astype(jnp.bfloat16)
    gv_out[...] = ends[1].astype(jnp.bfloat16)
    to_y.wait_recv()
    for h in range(heads):
        at = slice(h * HEAD, (h + 1) * HEAD)
        x = dq[1, at, :] * scale + first[1, at, :].astype(jnp.float32) + second[at, :].astype(jnp.float32)
        gq_out[:, at] = (x * cosine - pltpu.roll(x, HEAD // 2, 1) * sine).astype(jnp.bfloat16)

    for d in range(2):
        for a in range(1, far[d] + 1):
            pass_on(d, a, 0, 1).wait_send()
            give(d, a, stage.at[d, 0], 1).wait_send()
    for copy in (*copies, q_y, q_core, *forward, *small, *to_core, to_y):
        copy.wait_send()


def shards(queries, keys, values, attn_out, out_grad, logsumexp, position_ids, block_map, span_blocks):
    rows, width = queries.shape
    heads = width // HEAD
    nz = lax.axis_size("ctx") // QUAD
    ntp = lax.axis_size("tp")
    cosine, sine = rope_tables(position_ids)
    vmem = pl.BlockSpec(memory_space=pltpu.VMEM)
    smem = pl.BlockSpec(memory_space=pltpu.SMEM)
    hbm = pl.BlockSpec(memory_space=pl.ANY)
    dma = pltpu.SemaphoreType.DMA
    bf16, f32 = jnp.bfloat16, jnp.float32
    half = nz // 2
    tall = heads * HEAD
    return pl.pallas_call(
        functools.partial(step_kernel, nz, ntp),
        out_shape=(
            jax.ShapeDtypeStruct((rows, width), bf16),
            jax.ShapeDtypeStruct((rows, HEAD), bf16),
            jax.ShapeDtypeStruct((rows, HEAD), bf16),
        ),
        in_specs=[smem, smem, hbm, hbm, hbm, hbm, hbm, hbm, vmem, vmem],
        out_specs=(vmem, vmem, vmem),
        scratch_shapes=[
            pltpu.VMEM((rows, width), bf16),
            pltpu.VMEM((rows, width), bf16),
            pltpu.VMEM((heads, rows), f32),
            pltpu.VMEM((rows, HEAD), bf16),
            pltpu.VMEM((QUAD, tall, HEAD), bf16),
            pltpu.VMEM((QUAD, rows, width), bf16),
            pltpu.VMEM((QUAD, 2, heads, rows), f32),
            pltpu.VMEM((half, 2, 2 * rows, HEAD), bf16),
            pltpu.VMEM((half, 2, 2 * rows, HEAD), f32),
            pltpu.VMEM((2, 2 * tall, HEAD), f32),
            pltpu.VMEM((2, tall, HEAD), bf16),
            pltpu.VMEM((2, tall, HEAD), bf16),
            pltpu.VMEM((tall, HEAD), bf16),
            pltpu.VMEM((2, half + 1, 2, rows, HEAD), bf16),
            pltpu.VMEM((2, 2, 2, rows, HEAD), bf16),
            pltpu.VMEM((tall, HEAD), bf16),
            pltpu.VMEM((8, HEAD), jnp.int32),
            dma((6,)), dma((2, ntp)), dma((2, ntp)), dma((2, half + 1)), dma((2, half + 1)),
            dma((2,)), dma((2,)), dma((3,)), dma((3,)), dma((3,)), dma((3,)),
            dma((2, half + 1)), dma((2, half + 1)), dma((3,)), dma((3,)),
        ],
        compiler_params=pltpu.CompilerParams(
            vmem_limit_bytes=56 * 1024 * 1024, collective_id=0, has_side_effects=True
        ),
        name="attention_backward",
    )(
        block_map, span_blocks, queries, keys, values, attn_out, out_grad, logsumexp, cosine, sine
    )


def solution(mesh):
    return jax.shard_map(
        shards,
        mesh=mesh,
        in_specs=(
            P("ctx", "tp"),
            P("ctx", "tp"),
            P("ctx", "tp"),
            P("ctx", "tp"),
            P(("ctx", "tp"), None),
            P("tp", "ctx"),
            P(None, "ctx"),
            P(),
            P(),
        ),
        out_specs=(P("ctx", "tp"), P("ctx", "tp"), P("ctx", "tp")),
        check_vma=False,
    )
```

```python
import functools
import math

import jax
import jax.numpy as jnp
from jax import lax
from jax.experimental import pallas as pl
from jax.experimental.pallas import tpu as pltpu
from jax.sharding import PartitionSpec as P

HEAD = 128
BLK = 64
QUAD = 4
THETA = 1000000.0
LOG2E = 1.4426950408889634


def rope_tables(ids):
    half = HEAD // 2
    pair = lax.broadcasted_iota(jnp.int32, (half, HEAD), 0)
    inverse = jnp.exp(pair.astype(jnp.float32) * jnp.float32(-2.0 * math.log(THETA) / HEAD))
    first_cut = HEAD // 8
    second_cut = first_cut + 3 * HEAD // 16
    picked = jnp.where(pair < first_cut, ids[0:1, :], jnp.where(pair < second_cut, ids[1:2, :], ids[2:3, :]))
    angles = picked.astype(jnp.float32) * inverse
    cosine, sine = jnp.cos(angles), jnp.sin(angles)
    return jnp.concatenate([cosine, cosine], axis=0).T, jnp.concatenate([-sine, sine], axis=0).T


MESH = pl.DeviceIdType.MESH


def signal_all(barrier, peers):
    for peer in peers:
        pl.semaphore_signal(barrier, inc=1, device_id=peer, device_id_type=MESH)
    pl.semaphore_wait(barrier, len(peers))


def send(source, target, send_sem, recv_sem, peer):
    return pltpu.make_async_remote_copy(
        src_ref=source,
        dst_ref=target,
        send_sem=send_sem,
        recv_sem=recv_sem,
        device_id=peer,
        device_id_type=MESH,
    )


def step_kernel(
    nz, ntp, map_in, span_in, q_in, k_in, v_in, out_in, grad_in, lse_in, ids_in,
    all_out,
    q_raw, out_raw, lse_raw, k_raw, q_all, do_all, stats, kv, part, dq, dq_go, first, second, carry, stage, back, limits,
    local, do_send, do_recv, kv_send, kv_recv, q_send, q_recv, fwd_send, fwd_recv, st_send, st_recv,
    rs_send, rs_recv, dq_send, dq_recv,
):
    me = lax.axis_index("ctx")
    tp = lax.axis_index("tp")
    z, j = me // QUAD, me % QUAD
    yh, core = j // 2, j % 2
    rows, width = q_in.shape
    heads = width // HEAD
    slab = rows // ntp
    n = nz * QUAD
    half = nz // 2
    far = (half, half - 1)
    scale = 1.0 / math.sqrt(HEAD)
    at_core = me + 1 - 2 * core
    at_y = me + 2 - 4 * yh
    core_peer = {"ctx": at_core, "tp": tp}
    y_peer = {"ctx": at_y, "tp": tp}
    cross_peer = {"ctx": at_core + 2 - 4 * yh, "tp": tp}
    along = {k: {"ctx": (me + QUAD * k + n) % n, "tp": tp} for k in (1, 2, -1, -2)}

    loads = [
        pltpu.make_async_copy(source, target, local.at[i])
        for i, (source, target) in enumerate(
            ((k_in, k_raw), (v_in, kv.at[0, 1, pl.ds(rows, rows), :]), (q_in, q_raw), (out_in, out_raw), (lse_in, lse_raw))
        )
    ]
    for load in loads:
        load.start()
    cosine, sine = rope_tables(ids_in)
    others = [{"ctx": where, "tp": (tp + i) % ntp} for where in (me, at_y) for i in range(1, ntp)]
    signal_all(
        pltpu.get_barrier_semaphore(), [*along.values(), core_peer, y_peer, cross_peer, *others]
    )

    def shard(d, a):
        if a == 0 or a == half:
            return kv.at[0, :, pl.ds(rows if a == 0 else 0, rows), :]
        return kv.at[a, :, pl.ds(rows if d == 0 else 0, rows), :]

    def pass_on(d, a, from_a, places):
        return send(
            shard(d, from_a), shard(d, a), kv_send.at[d, a], kv_recv.at[d, a], along[places if d == 0 else -places]
        )

    def arrived(a):
        for d in range(2):
            if a <= far[d]:
                pass_on(d, a, a, 1).wait_recv()
            if a + 2 <= far[d]:
                pass_on(d, a + 2, a, 2).start()

    loads[0].wait()
    loads[1].wait()
    k = k_raw[...].astype(jnp.float32)
    kv[0, 0, rows : 2 * rows, :] = (k * cosine + pltpu.roll(k, HEAD // 2, 1) * sine).astype(jnp.bfloat16)
    for a in (2, 1):
        for d in range(2):
            if a <= far[d]:
                pass_on(d, a, 0, a).start()

    mine = pl.ds(pl.multiple_of(tp * slab, slab), slab)
    copies = []
    own = None
    for i in range(ntp):
        t = (tp + i) % ntp
        piece = grad_in.at[:, pl.ds(pl.multiple_of(t * width, width), width)]
        for a, where in enumerate((me, at_y)):
            if i == 0 and a == 0:
                own = pltpu.make_async_copy(piece, do_all.at[2, mine, :], local.at[5])
                own.start()
            else:
                slot = 2 if a == 0 else 0
                copies.append(
                    send(piece, do_all.at[slot, mine, :], do_send.at[a, i], do_recv.at[a, i], {"ctx": where, "tp": t})
                )
                copies[-1].start()

    loads[2].wait()
    for h in range(heads):
        at = slice(h * HEAD, (h + 1) * HEAD)
        x = q_raw[:, at].astype(jnp.float32)
        q_all[2, at, :] = (x * cosine + pltpu.roll(x, HEAD // 2, 1) * sine).astype(jnp.bfloat16)
    q_y = send(q_all.at[2], q_all.at[0], q_send.at[0], q_recv.at[0], y_peer)
    q_core = send(q_all.at[2], q_all.at[3], q_send.at[1], q_recv.at[1], core_peer)
    q_y.start()
    q_core.start()

    lane = lax.broadcasted_iota(jnp.int32, (1, HEAD), 1)
    dq[...] = jnp.zeros_like(dq)

    def limit_of(block):
        place = map_in[block]
        end = jnp.int32(0)
        for i in range(span_in.shape[1]):
            inside = (place >= span_in[0, i]) & (place < span_in[1, i])
            end = end + jnp.where(inside, span_in[1, i], 0)
        return place * BLK, end * BLK - 1

    for slot, member in enumerate((j + 2 - 4 * yh, (j + 2 - 4 * yh) + 1 - 2 * core, j, j + 1 - 2 * core)):
        pieces = []
        for b in range(2):
            place, end = limit_of((z * QUAD + member) * 2 + b)
            pieces.append(jnp.maximum(place + lane - b * BLK, end))
        limits[slot : slot + 1, :] = jnp.where(lane < BLK, pieces[0], pieces[1])
    arrived(1)
    for a in range(2, min(4, half - 1)):
        arrived(a)

    def from_slot(slot, axis, i):
        t = (tp - i + ntp) % ntp
        there = do_all.at[slot, pl.ds(pl.multiple_of(t * slab, slab), slab), :]
        return send(there, there, do_send.at[axis, i], do_recv.at[axis, i], core_peer)

    own.wait()
    for i in range(1, ntp):
        from_slot(2, 0, i).wait_recv()
    forward = [send(do_all.at[2], do_all.at[3], fwd_send.at[0], fwd_recv.at[0], core_peer)]
    forward[0].start()
    loads[3].wait()
    loads[4].wait()
    for h in range(heads):
        at = slice(h * HEAD, (h + 1) * HEAD)
        product = do_all[2, :, at].astype(jnp.float32) * out_raw[:, at].astype(jnp.float32)
        stats[2, 0, h : h + 1, :] = lse_raw[h : h + 1, :] * LOG2E
        stats[2, 1, h : h + 1, :] = jnp.sum(product.T, axis=0, keepdims=True)
    small = [
        send(stats.at[2], stats.at[slot], st_send.at[i], st_recv.at[i], peer)
        for i, (slot, peer) in enumerate(((3, core_peer), (0, y_peer), (1, cross_peer)))
    ]
    for copy in small:
        copy.start()
    q_y.wait_recv()
    forward.append(send(q_all.at[0], q_all.at[1], fwd_send.at[1], fwd_recv.at[1], core_peer))
    forward[1].start()
    for a in range(4, half - 1):
        arrived(a)
    for i in range(ntp):
        from_slot(0, 1, i).wait_recv()
    forward.append(send(do_all.at[0], do_all.at[1], fwd_send.at[2], fwd_recv.at[2], core_peer))
    forward[2].start()
    for copy in (q_core, *forward, *small):
        copy.wait_recv()

    sub = lax.broadcasted_iota(jnp.int32, (BLK, HEAD), 0)

    def unit(p, g, keep_part):
        kp, vp = kv[p, 0], kv[p, 1]
        slots = (2 * g, 2 * g + 1)
        qs = jnp.concatenate([q_all[slot] for slot in slots], axis=0)
        grads = jnp.concatenate(
            [do_all[slot, :, h * HEAD : (h + 1) * HEAD] for slot in slots for h in range(heads)], axis=0
        )
        up = (p + half - 1) % half + 1
        shards_z = ((z + up) % nz, (z - p + nz) % nz)
        places = [map_in[(s * QUAD + j) * 2 + b] * BLK for s in shards_z for b in range(2)]
        s = lax.dot_general(kp, qs, (((1,), (1,)), ((), ())), preferred_element_type=jnp.float32)
        dp = lax.dot_general(vp, grads, (((1,), (1,)), ((), ())), preferred_element_type=jnp.float32)
        probs, scores = [], []
        for i, slot in enumerate(slots):
            bound = limits[slot : slot + 1, :]
            allowed = jnp.concatenate([sub <= bound - place for place in places], axis=0)
            for h in range(heads):
                at = slice((i * heads + h) * HEAD, (i * heads + h + 1) * HEAD)
                x = s[:, at] * (scale * LOG2E) - stats[slot, 0, h : h + 1, :]
                prob = jnp.exp2(jnp.where(allowed, x, -jnp.inf))
                probs.append(prob.astype(jnp.bfloat16))
                scores.append((prob * (dp[:, at] - stats[slot, 1, h : h + 1, :])).astype(jnp.bfloat16))
        probs = jnp.concatenate(probs, axis=1)
        scores = jnp.concatenate(scores, axis=1)
        dv = jnp.dot(probs, grads, preferred_element_type=jnp.float32)
        dk = jnp.dot(scores, qs, preferred_element_type=jnp.float32) * scale
        if keep_part:
            part[p, 0] += dk
            part[p, 1] += dv
        else:
            part[p, 0] = dk
            part[p, 1] = dv
        dq[g] += lax.dot_general(scores, kp, (((0,), (0,)), ((), ())), preferred_element_type=jnp.float32)

    def part_of(d, s, p):
        return part[p, :, (0 if d == 0 else rows) : (rows if d == 0 else 2 * rows), :]

    def give(d, s, source, places):
        return send(
            source, carry.at[d, s], rs_send.at[d, s], rs_recv.at[d, s], along[places if d == 0 else -places]
        )

    def start_chain(d, s, p, places):
        at = far[d] - s
        stage[d, at] = part_of(d, s, p).astype(jnp.bfloat16)
        give(d, s, stage.at[d, at], places).start()

    def add_and_give(d, s, p, places):
        give(d, s + 2, carry.at[d, s + 2], 1).wait_recv()
        carry[d, s + 2] = (carry[d, s + 2].astype(jnp.float32) + part_of(d, s, p)).astype(jnp.bfloat16)
        give(d, s, carry.at[d, s + 2], places).start()

    to_core = [send(dq_go.at[i], first.at[i], dq_send.at[i], dq_recv.at[i], core_peer) for i in range(2)]
    span_rows = heads * HEAD
    near = 2 if half >= 4 else 1

    def one_pair(i, unused):
        late = (i + half - near) // half
        s = half + near - i
        p = (1 - late) * (i + 1) + late * (s % half)

        @pl.when(i == near)
        def _():
            pass_on(0, half, half, 1).wait_recv()

        if half - 1 > 1:

            @pl.when(i == near + 1)
            def _():
                arrived(half - 1)

        unit(p, 0, False)

        @pl.when(i == half - 1)
        def _():
            dq_go[0] = (dq[0, span_rows : 2 * span_rows, :] * scale).astype(jnp.bfloat16)
            to_core[0].start()

        unit(p, 1, True)
        for d in range(2):

            @pl.when((i >= near + d) & (i <= near + 1 + d))
            def _():
                start_chain(d, s, p, 2)

            if half > near + 2 + d:

                @pl.when(i >= near + 2 + d)
                def _():
                    add_and_give(d, s, p, 2)

        return unused

    lax.fori_loop(0, half, one_pair, 0)
    dq_go[1] = (dq[1, span_rows : 2 * span_rows, :] * scale).astype(jnp.bfloat16)
    to_core[1].start()
    to_core[0].wait_recv()
    back[...] = (dq[0, 0:span_rows, :] * scale + first[0].astype(jnp.float32)).astype(jnp.bfloat16)
    to_y = send(back, second, dq_send.at[2], dq_recv.at[2], y_peer)
    to_y.start()
    for s in range(near, 0, -1):
        for d in range(2):
            if s + 2 <= far[d]:
                add_and_give(d, s, s, min(s, 2))
            elif s <= far[d]:
                start_chain(d, s, s, min(s, 2))
    to_core[1].wait_recv()
    ends = [part[0, what, rows : 2 * rows, :] for what in range(2)]
    for d in range(2):
        for s in (2, 1):
            if s <= far[d]:
                give(d, s, carry.at[d, s], 1).wait_recv()
                ends = [ends[what] + carry[d, s, what].astype(jnp.float32) for what in range(2)]
    all_out[:, width : width + HEAD] = (ends[0] * cosine - pltpu.roll(ends[0], HEAD // 2, 1) * sine).astype(jnp.bfloat16)
    all_out[:, width + HEAD :] = ends[1].astype(jnp.bfloat16)
    to_y.wait_recv()
    for h in range(heads):
        at = slice(h * HEAD, (h + 1) * HEAD)
        x = dq[1, at, :] * scale + first[1, at, :].astype(jnp.float32) + second[at, :].astype(jnp.float32)
        all_out[:, at] = (x * cosine - pltpu.roll(x, HEAD // 2, 1) * sine).astype(jnp.bfloat16)

    for d in range(2):
        for a in range(1, far[d] + 1):
            pass_on(d, a, 0, 1).wait_send()
            give(d, a, stage.at[d, 0], 1).wait_send()
    for copy in (*copies, q_y, q_core, *forward, *small, *to_core, to_y):
        copy.wait_send()


def shards(queries, keys, values, attn_out, out_grad, logsumexp, position_ids, block_map, span_blocks):
    rows, width = queries.shape
    heads = width // HEAD
    nz = lax.axis_size("ctx") // QUAD
    ntp = lax.axis_size("tp")
    vmem = pl.BlockSpec(memory_space=pltpu.VMEM)
    smem = pl.BlockSpec(memory_space=pltpu.SMEM)
    hbm = pl.BlockSpec(memory_space=pl.ANY)
    dma = pltpu.SemaphoreType.DMA
    bf16, f32 = jnp.bfloat16, jnp.float32
    half = nz // 2
    tall = heads * HEAD
    together = pl.pallas_call(
        functools.partial(step_kernel, nz, ntp),
        out_shape=jax.ShapeDtypeStruct((rows, width + 2 * HEAD), bf16),
        in_specs=[smem, smem, hbm, hbm, hbm, hbm, hbm, hbm, vmem],
        out_specs=vmem,
        scratch_shapes=[
            pltpu.VMEM((rows, width), bf16),
            pltpu.VMEM((rows, width), bf16),
            pltpu.VMEM((heads, rows), f32),
            pltpu.VMEM((rows, HEAD), bf16),
            pltpu.VMEM((QUAD, tall, HEAD), bf16),
            pltpu.VMEM((QUAD, rows, width), bf16),
            pltpu.VMEM((QUAD, 2, heads, rows), f32),
            pltpu.VMEM((half, 2, 2 * rows, HEAD), bf16),
            pltpu.VMEM((half, 2, 2 * rows, HEAD), f32),
            pltpu.VMEM((2, 2 * tall, HEAD), f32),
            pltpu.VMEM((2, tall, HEAD), bf16),
            pltpu.VMEM((2, tall, HEAD), bf16),
            pltpu.VMEM((tall, HEAD), bf16),
            pltpu.VMEM((2, half + 1, 2, rows, HEAD), bf16),
            pltpu.VMEM((2, 2, 2, rows, HEAD), bf16),
            pltpu.VMEM((tall, HEAD), bf16),
            pltpu.VMEM((8, HEAD), jnp.int32),
            dma((6,)), dma((2, ntp)), dma((2, ntp)), dma((2, half + 1)), dma((2, half + 1)),
            dma((2,)), dma((2,)), dma((3,)), dma((3,)), dma((3,)), dma((3,)),
            dma((2, half + 1)), dma((2, half + 1)), dma((3,)), dma((3,)),
        ],
        compiler_params=pltpu.CompilerParams(
            vmem_limit_bytes=56 * 1024 * 1024, collective_id=0, has_side_effects=True
        ),
        name="attention_backward",
    )(
        block_map, span_blocks.T, queries, keys, values, attn_out, out_grad, logsumexp, position_ids
    )
    return together[:, :width], together[:, width : width + HEAD], together[:, width + HEAD :]


def solution(mesh):
    return jax.shard_map(
        shards,
        mesh=mesh,
        in_specs=(
            P("ctx", "tp"),
            P("ctx", "tp"),
            P("ctx", "tp"),
            P("ctx", "tp"),
            P(("ctx", "tp"), None),
            P("tp", "ctx"),
            P(None, "ctx"),
            P(),
            P(),
        ),
        out_specs=(P("ctx", "tp"), P("ctx", "tp"), P("ctx", "tp")),
        check_vma=False,
    )
```

```python
import functools
import math

import jax
import jax.numpy as jnp
from jax import lax
from jax.experimental import pallas as pl
from jax.experimental.pallas import tpu as pltpu
from jax.sharding import PartitionSpec as P

HEAD = 128
BLK = 64
QUAD = 4
THETA = 1000000.0
LOG2E = 1.4426950408889634


def rope_tables(ids):
    half = HEAD // 2
    pair = lax.broadcasted_iota(jnp.int32, (half, HEAD), 0)
    inverse = jnp.exp(pair.astype(jnp.float32) * jnp.float32(-2.0 * math.log(THETA) / HEAD))
    first_cut = HEAD // 8
    second_cut = first_cut + 3 * HEAD // 16
    picked = jnp.where(pair < first_cut, ids[0:1, :], jnp.where(pair < second_cut, ids[1:2, :], ids[2:3, :]))
    angles = picked.astype(jnp.float32) * inverse
    cosine, sine = jnp.cos(angles), jnp.sin(angles)
    return jnp.concatenate([cosine, cosine], axis=0).T, jnp.concatenate([-sine, sine], axis=0).T


MESH = pl.DeviceIdType.MESH


def signal_all(barrier, peers):
    for peer in peers:
        pl.semaphore_signal(barrier, inc=1, device_id=peer, device_id_type=MESH)


def send(source, target, send_sem, recv_sem, peer):
    return pltpu.make_async_remote_copy(
        src_ref=source,
        dst_ref=target,
        send_sem=send_sem,
        recv_sem=recv_sem,
        device_id=peer,
        device_id_type=MESH,
    )


def step_kernel(
    nz, ntp, map_in, span_in, q_in, k_in, v_in, out_in, grad_in, lse_in, ids_in,
    all_out,
    q_raw, out_raw, lse_raw, k_raw, q_all, do_all, stats, kv, part, dq, dq_go, first, second, carry, stage, back, limits,
    local, do_send, do_recv, kv_send, kv_recv, q_send, q_recv, fwd_send, fwd_recv, st_send, st_recv,
    rs_send, rs_recv, dq_send, dq_recv,
):
    me = lax.axis_index("ctx")
    tp = lax.axis_index("tp")
    z, j = me // QUAD, me % QUAD
    yh, core = j // 2, j % 2
    rows, width = q_in.shape
    heads = width // HEAD
    slab = rows // ntp
    n = nz * QUAD
    half = nz // 2
    far = (half, half - 1)
    scale = 1.0 / math.sqrt(HEAD)
    at_core = me + 1 - 2 * core
    at_y = me + 2 - 4 * yh
    core_peer = {"ctx": at_core, "tp": tp}
    y_peer = {"ctx": at_y, "tp": tp}
    cross_peer = {"ctx": at_core + 2 - 4 * yh, "tp": tp}
    along = {k: {"ctx": (me + QUAD * k + n) % n, "tp": tp} for k in (1, 2, -1, -2)}

    loads = [
        pltpu.make_async_copy(source, target, local.at[i])
        for i, (source, target) in enumerate(
            ((k_in, k_raw), (v_in, kv.at[0, 1, pl.ds(rows, rows), :]), (q_in, q_raw), (out_in, out_raw), (lse_in, lse_raw))
        )
    ]
    for load in loads:
        load.start()
    others = [{"ctx": where, "tp": (tp + i) % ntp} for where in (me, at_y) for i in range(1, ntp)]
    peers = [*along.values(), core_peer, y_peer, cross_peer, *others]
    barrier = pltpu.get_barrier_semaphore()
    signal_all(barrier, peers)
    cosine, sine = rope_tables(ids_in)
    lane = lax.broadcasted_iota(jnp.int32, (1, HEAD), 1)
    dq[...] = jnp.zeros_like(dq)
    part[...] = jnp.zeros_like(part)

    def limit_of(block):
        place = map_in[block]
        end = jnp.int32(0)
        for i in range(span_in.shape[1]):
            inside = (place >= span_in[0, i]) & (place < span_in[1, i])
            end = end + jnp.where(inside, span_in[1, i], 0)
        return place * BLK, end * BLK - 1

    for slot, member in enumerate((j + 2 - 4 * yh, (j + 2 - 4 * yh) + 1 - 2 * core, j, j + 1 - 2 * core)):
        pieces = []
        for b in range(2):
            place, end = limit_of((z * QUAD + member) * 2 + b)
            pieces.append(jnp.maximum(place + lane - b * BLK, end))
        limits[slot] = jnp.where(lane < BLK, pieces[0], pieces[1])
    pl.semaphore_wait(barrier, len(peers))

    def shard(d, a):
        if a == 0 or a == half:
            return kv.at[0, :, pl.ds(rows if a == 0 else 0, rows), :]
        return kv.at[a, :, pl.ds(rows if d == 0 else 0, rows), :]

    def pass_on(d, a, from_a, places):
        return send(
            shard(d, from_a), shard(d, a), kv_send.at[d, a], kv_recv.at[d, a], along[places if d == 0 else -places]
        )

    def arrived(a):
        for d in range(2):
            if a <= far[d]:
                pass_on(d, a, a, 1).wait_recv()
            if a + 2 <= far[d]:
                pass_on(d, a + 2, a, 2).start()

    loads[0].wait()
    loads[1].wait()
    k = k_raw[...].astype(jnp.float32)
    kv[0, 0, rows : 2 * rows, :] = (k * cosine + pltpu.roll(k, HEAD // 2, 1) * sine).astype(jnp.bfloat16)
    for a in (2, 1):
        for d in range(2):
            if a <= far[d]:
                pass_on(d, a, 0, a).start()

    mine = pl.ds(pl.multiple_of(tp * slab, slab), slab)
    copies = []
    own = None
    for i in range(ntp):
        t = (tp + i) % ntp
        piece = grad_in.at[:, pl.ds(pl.multiple_of(t * width, width), width)]
        for a, where in enumerate((me, at_y)):
            if i == 0 and a == 0:
                own = pltpu.make_async_copy(piece, do_all.at[2, mine, :], local.at[5])
                own.start()
            else:
                slot = 2 if a == 0 else 0
                copies.append(
                    send(piece, do_all.at[slot, mine, :], do_send.at[a, i], do_recv.at[a, i], {"ctx": where, "tp": t})
                )
                copies[-1].start()

    loads[2].wait()
    for h in range(heads):
        at = slice(h * HEAD, (h + 1) * HEAD)
        x = q_raw[:, at].astype(jnp.float32)
        q_all[2, at, :] = (x * cosine + pltpu.roll(x, HEAD // 2, 1) * sine).astype(jnp.bfloat16)
    q_y = send(q_all.at[2], q_all.at[0], q_send.at[0], q_recv.at[0], y_peer)
    q_core = send(q_all.at[2], q_all.at[3], q_send.at[1], q_recv.at[1], core_peer)
    q_y.start()
    q_core.start()

    arrived(1)
    near = 3 if half >= 8 else (2 if half >= 4 else 1)
    for a in range(2, near + 1):
        arrived(a)
    later = list(range(near + 1, half - 1))

    def from_slot(slot, axis, i):
        t = (tp - i + ntp) % ntp
        there = do_all.at[slot, pl.ds(pl.multiple_of(t * slab, slab), slab), :]
        return send(there, there, do_send.at[axis, i], do_recv.at[axis, i], core_peer)

    own.wait()
    for i in range(1, ntp):
        from_slot(2, 0, i).wait_recv()
    forward = [send(do_all.at[2], do_all.at[3], fwd_send.at[0], fwd_recv.at[0], core_peer)]
    forward[0].start()
    loads[3].wait()
    loads[4].wait()
    for h in range(heads):
        at = slice(h * HEAD, (h + 1) * HEAD)
        product = do_all[2, :, at].astype(jnp.float32) * out_raw[:, at].astype(jnp.float32)
        stats[2, 0, h : h + 1, :] = lse_raw[h : h + 1, :] * LOG2E
        stats[2, 1, h : h + 1, :] = jnp.sum(product.T, axis=0, keepdims=True)
    small = [
        send(stats.at[2], stats.at[slot], st_send.at[i], st_recv.at[i], peer)
        for i, (slot, peer) in enumerate(((3, core_peer), (0, y_peer), (1, cross_peer)))
    ]
    for copy in small:
        copy.start()
    q_y.wait_recv()
    forward.append(send(q_all.at[0], q_all.at[1], fwd_send.at[1], fwd_recv.at[1], core_peer))
    forward[1].start()
    if later:
        arrived(later[0])
    forward.append(send(do_all.at[0], do_all.at[1], fwd_send.at[2], fwd_recv.at[2], core_peer))
    for copy in (q_core, forward[0], small[0]):
        copy.wait_recv()

    sub = lax.broadcasted_iota(jnp.int32, (BLK, HEAD), 0)

    def unit(p, g):
        kp, vp = kv[p, 0], kv[p, 1]
        slots = (2 * g, 2 * g + 1)
        qs = jnp.concatenate([q_all[slot] for slot in slots], axis=0)
        grads = jnp.concatenate(
            [do_all[slot, :, h * HEAD : (h + 1) * HEAD] for slot in slots for h in range(heads)], axis=0
        )
        up = (p + half - 1) % half + 1
        shards_z = ((z + up) % nz, (z - p + nz) % nz)
        places = [map_in[(s * QUAD + j) * 2 + b] * BLK for s in shards_z for b in range(2)]
        s = lax.dot_general(kp, qs, (((1,), (1,)), ((), ())), preferred_element_type=jnp.float32)
        dp = lax.dot_general(vp, grads, (((1,), (1,)), ((), ())), preferred_element_type=jnp.float32)
        probs, scores = [], []
        for i, slot in enumerate(slots):
            bound = limits[slot]
            allowed = jnp.concatenate([sub <= bound - place for place in places], axis=0)
            for h in range(heads):
                at = slice((i * heads + h) * HEAD, (i * heads + h + 1) * HEAD)
                x = s[:, at] * (scale * LOG2E) - stats[slot, 0, h : h + 1, :]
                prob = jnp.exp2(jnp.where(allowed, x, -jnp.inf))
                probs.append(prob.astype(jnp.bfloat16))
                scores.append((prob * (dp[:, at] - stats[slot, 1, h : h + 1, :])).astype(jnp.bfloat16))
        probs = jnp.concatenate(probs, axis=1)
        scores = jnp.concatenate(scores, axis=1)
        dv = jnp.dot(probs, grads, preferred_element_type=jnp.float32)
        dk = jnp.dot(scores, qs, preferred_element_type=jnp.float32) * scale
        part[p, 0] += dk
        part[p, 1] += dv
        dq[g] += lax.dot_general(scores, kp, (((0,), (0,)), ((), ())), preferred_element_type=jnp.float32)

    def part_of(d, s, p):
        return part[p, :, (0 if d == 0 else rows) : (rows if d == 0 else 2 * rows), :]

    def give(d, s, source, places):
        return send(
            source, carry.at[d, s], rs_send.at[d, s], rs_recv.at[d, s], along[places if d == 0 else -places]
        )

    def start_chain(d, s, p, places):
        at = far[d] - s
        stage[d, at] = part_of(d, s, p).astype(jnp.bfloat16)
        give(d, s, stage.at[d, at], places).start()

    def add_and_give(d, s, p, places):
        give(d, s + 2, carry.at[d, s + 2], 1).wait_recv()
        carry[d, s + 2] = (carry[d, s + 2].astype(jnp.float32) + part_of(d, s, p)).astype(jnp.bfloat16)
        give(d, s, carry.at[d, s + 2], places).start()

    to_core = [send(dq_go.at[i], first.at[i], dq_send.at[i], dq_recv.at[i], core_peer) for i in range(2)]
    span_rows = heads * HEAD

    def one_unit(u, unused):
        late = (u + 2 * half - 2 * near) // (2 * half)
        order = (u + 2 * half - 2 * near) % (2 * half) // 2
        s = half - order
        p = (1 - late) * (u % near + 1) + late * (s % half)
        g = (1 - late) * (1 - u // near % 2) + late * (u % 2)

        @pl.when(u == 2 * near)
        def _():
            pass_on(0, half, half, 1).wait_recv()

        if half - 1 > near:

            @pl.when(u == 2 * near + 2)
            def _():
                arrived(half - 1)

        unit(p, g)

        @pl.when(u == 0)
        def _():
            if len(later) > 1:
                arrived(later[1])
            for i in range(ntp):
                from_slot(0, 1, i).wait_recv()
            forward[2].start()

        if len(later) > 2:

            @pl.when(u == 1)
            def _():
                arrived(later[2])

        @pl.when(u == near - 1)
        def _():
            for copy in (*forward[1:], *small[1:]):
                copy.wait_recv()

        @pl.when(u == 2 * half - 2)
        def _():
            dq_go[0] = (dq[0, span_rows : 2 * span_rows, :] * scale).astype(jnp.bfloat16)
            to_core[0].start()

        for d in range(2):
            first_of = 2 * near + 2 * d + 1

            @pl.when((u == first_of) | (u == first_of + 2))
            def _():
                start_chain(d, s, p, 2)

            if 2 * half > first_of + 4:

                @pl.when((u >= first_of + 4) & (u % 2 == 1))
                def _():
                    add_and_give(d, s, p, 2)

        return unused

    lax.fori_loop(0, 2 * half, one_unit, 0)
    dq_go[1] = (dq[1, span_rows : 2 * span_rows, :] * scale).astype(jnp.bfloat16)
    to_core[1].start()
    to_core[0].wait_recv()
    back[...] = (dq[0, 0:span_rows, :] * scale + first[0].astype(jnp.float32)).astype(jnp.bfloat16)
    to_y = send(back, second, dq_send.at[2], dq_recv.at[2], y_peer)
    to_y.start()
    for s in range(near, 0, -1):
        for d in range(2):
            if s + 2 <= far[d]:
                add_and_give(d, s, s, min(s, 2))
            elif s <= far[d]:
                start_chain(d, s, s, min(s, 2))
    to_core[1].wait_recv()
    ends = [part[0, what, rows : 2 * rows, :] for what in range(2)]
    for d in range(2):
        for s in (2, 1):
            if s <= far[d]:
                give(d, s, carry.at[d, s], 1).wait_recv()
                ends = [ends[what] + carry[d, s, what].astype(jnp.float32) for what in range(2)]
    all_out[:, width : width + HEAD] = (ends[0] * cosine - pltpu.roll(ends[0], HEAD // 2, 1) * sine).astype(jnp.bfloat16)
    all_out[:, width + HEAD :] = ends[1].astype(jnp.bfloat16)
    to_y.wait_recv()
    for h in range(heads):
        at = slice(h * HEAD, (h + 1) * HEAD)
        x = dq[1, at, :] * scale + first[1, at, :].astype(jnp.float32) + second[at, :].astype(jnp.float32)
        all_out[:, at] = (x * cosine - pltpu.roll(x, HEAD // 2, 1) * sine).astype(jnp.bfloat16)

    for d in range(2):
        for a in range(1, far[d] + 1):
            pass_on(d, a, 0, 1).wait_send()
            give(d, a, stage.at[d, 0], 1).wait_send()
    for copy in (*copies, q_y, q_core, *forward, *small, *to_core, to_y):
        copy.wait_send()


def shards(queries, keys, values, attn_out, out_grad, logsumexp, position_ids, block_map, span_blocks):
    rows, width = queries.shape
    heads = width // HEAD
    nz = lax.axis_size("ctx") // QUAD
    ntp = lax.axis_size("tp")
    vmem = pl.BlockSpec(memory_space=pltpu.VMEM)
    smem = pl.BlockSpec(memory_space=pltpu.SMEM)
    hbm = pl.BlockSpec(memory_space=pl.ANY)
    dma = pltpu.SemaphoreType.DMA
    bf16, f32 = jnp.bfloat16, jnp.float32
    half = nz // 2
    tall = heads * HEAD
    together = pl.pallas_call(
        functools.partial(step_kernel, nz, ntp),
        out_shape=jax.ShapeDtypeStruct((rows, width + 2 * HEAD), bf16),
        in_specs=[smem, smem, hbm, hbm, hbm, hbm, hbm, hbm, vmem],
        out_specs=vmem,
        scratch_shapes=[
            pltpu.VMEM((rows, width), bf16),
            pltpu.VMEM((rows, width), bf16),
            pltpu.VMEM((heads, rows), f32),
            pltpu.VMEM((rows, HEAD), bf16),
            pltpu.VMEM((QUAD, tall, HEAD), bf16),
            pltpu.VMEM((QUAD, rows, width), bf16),
            pltpu.VMEM((QUAD, 2, heads, rows), f32),
            pltpu.VMEM((half, 2, 2 * rows, HEAD), bf16),
            pltpu.VMEM((half, 2, 2 * rows, HEAD), f32),
            pltpu.VMEM((2, 2 * tall, HEAD), f32),
            pltpu.VMEM((2, tall, HEAD), bf16),
            pltpu.VMEM((2, tall, HEAD), bf16),
            pltpu.VMEM((tall, HEAD), bf16),
            pltpu.VMEM((2, half + 1, 2, rows, HEAD), bf16),
            pltpu.VMEM((2, 2, 2, rows, HEAD), bf16),
            pltpu.VMEM((tall, HEAD), bf16),
            pltpu.VMEM((QUAD, 1, HEAD), jnp.int32),
            dma((6,)), dma((2, ntp)), dma((2, ntp)), dma((2, half + 1)), dma((2, half + 1)),
            dma((2,)), dma((2,)), dma((3,)), dma((3,)), dma((3,)), dma((3,)),
            dma((2, half + 1)), dma((2, half + 1)), dma((3,)), dma((3,)),
        ],
        compiler_params=pltpu.CompilerParams(
            vmem_limit_bytes=56 * 1024 * 1024, collective_id=0, has_side_effects=True
        ),
        name="attention_backward",
    )(
        block_map, span_blocks.T, queries, keys, values, attn_out, out_grad, logsumexp, position_ids
    )
    return together[:, :width], together[:, width : width + HEAD], together[:, width + HEAD :]


def solution(mesh):
    return jax.shard_map(
        shards,
        mesh=mesh,
        in_specs=(
            P("ctx", "tp"),
            P("ctx", "tp"),
            P("ctx", "tp"),
            P("ctx", "tp"),
            P(("ctx", "tp"), None),
            P("tp", "ctx"),
            P(None, "ctx"),
            P(),
            P(),
        ),
        out_specs=(P("ctx", "tp"), P("ctx", "tp"), P("ctx", "tp")),
        check_vma=False,
    )
```

```python
import functools
import math

import jax
import jax.numpy as jnp
from jax import lax
from jax.experimental import pallas as pl
from jax.experimental.pallas import tpu as pltpu
from jax.sharding import PartitionSpec as P

HEAD = 128
BLK = 64
QUAD = 4
THETA = 1000000.0
LOG2E = 1.4426950408889634


def rope_tables(ids):
    half = HEAD // 2
    pair = lax.broadcasted_iota(jnp.int32, (half, HEAD), 0)
    inverse = jnp.exp(pair.astype(jnp.float32) * jnp.float32(-2.0 * math.log(THETA) / HEAD))
    first_cut = HEAD // 8
    second_cut = first_cut + 3 * HEAD // 16
    picked = jnp.where(pair < first_cut, ids[0:1, :], jnp.where(pair < second_cut, ids[1:2, :], ids[2:3, :]))
    angles = picked.astype(jnp.float32) * inverse
    cosine, sine = jnp.cos(angles), jnp.sin(angles)
    return jnp.concatenate([cosine, cosine], axis=0).T, jnp.concatenate([-sine, sine], axis=0).T


MESH = pl.DeviceIdType.MESH


def signal_all(barrier, peers):
    for peer in peers:
        pl.semaphore_signal(barrier, inc=1, device_id=peer, device_id_type=MESH)


def send(source, target, send_sem, recv_sem, peer):
    return pltpu.make_async_remote_copy(
        src_ref=source,
        dst_ref=target,
        send_sem=send_sem,
        recv_sem=recv_sem,
        device_id=peer,
        device_id_type=MESH,
    )


def step_kernel(
    nz, ntp, map_in, span_in, q_in, k_in, v_in, out_in, grad_in, lse_in, ids_in,
    all_out,
    q_raw, out_raw, lse_raw, k_raw, q_all, do_all, stats, kv, part, dq, dq_go, first, second, carry, stage, back, limits,
    local, do_send, do_recv, kv_send, kv_recv, q_send, q_recv, fwd_send, fwd_recv, st_send, st_recv,
    rs_send, rs_recv, dq_send, dq_recv,
):
    me = lax.axis_index("ctx")
    tp = lax.axis_index("tp")
    z, j = me // QUAD, me % QUAD
    yh, core = j // 2, j % 2
    rows, width = q_in.shape
    heads = width // HEAD
    slab = rows // ntp
    n = nz * QUAD
    half = nz // 2
    far = (half, half - 1)
    scale = 1.0 / math.sqrt(HEAD)
    at_core = me + 1 - 2 * core
    at_y = me + 2 - 4 * yh
    core_peer = {"ctx": at_core, "tp": tp}
    y_peer = {"ctx": at_y, "tp": tp}
    cross_peer = {"ctx": at_core + 2 - 4 * yh, "tp": tp}
    near = 3 if half >= 8 else 2
    along = {k: {"ctx": (me + QUAD * k + n) % n, "tp": tp} for i in range(1, near + 3) for k in (i, -i)}

    loads = [
        pltpu.make_async_copy(source, target, local.at[i])
        for i, (source, target) in enumerate(
            ((k_in, k_raw), (v_in, kv.at[0, 1, pl.ds(rows, rows), :]), (q_in, q_raw), (out_in, out_raw), (lse_in, lse_raw))
        )
    ]
    for load in loads:
        load.start()
    others = [{"ctx": where, "tp": (tp + i) % ntp} for where in (me, at_y) for i in range(1, ntp)]
    peers = [*along.values(), core_peer, y_peer, cross_peer, *others]
    barrier = pltpu.get_barrier_semaphore()
    signal_all(barrier, peers)
    cosine, sine = rope_tables(ids_in)
    lane = lax.broadcasted_iota(jnp.int32, (1, HEAD), 1)
    dq[...] = jnp.zeros_like(dq)
    part[...] = jnp.zeros_like(part)

    def limit_of(block):
        place = map_in[block]
        end = jnp.int32(0)
        for i in range(span_in.shape[1]):
            inside = (place >= span_in[0, i]) & (place < span_in[1, i])
            end = end + jnp.where(inside, span_in[1, i], 0)
        return place * BLK, end * BLK - 1

    for slot, member in enumerate((j + 2 - 4 * yh, (j + 2 - 4 * yh) + 1 - 2 * core, j, j + 1 - 2 * core)):
        pieces = []
        for b in range(2):
            place, end = limit_of((z * QUAD + member) * 2 + b)
            pieces.append(jnp.maximum(place + lane - b * BLK, end))
        limits[slot] = jnp.where(lane < BLK, pieces[0], pieces[1])
    pl.semaphore_wait(barrier, len(peers))

    def shard(d, a):
        if a == 0 or a == half:
            return kv.at[0, :, pl.ds(rows if a == 0 else 0, rows), :]
        return kv.at[a, :, pl.ds(rows if d == 0 else 0, rows), :]

    def pass_on(d, a, from_a, places):
        return send(
            shard(d, from_a), shard(d, a), kv_send.at[d, a], kv_recv.at[d, a], along[places if d == 0 else -places]
        )

    def arrived(a):
        for d in range(2):
            if a <= far[d]:
                pass_on(d, a, a, 1).wait_recv()
            if a + 2 <= far[d]:
                pass_on(d, a + 2, a, 2).start()

    loads[0].wait()
    loads[1].wait()
    k = k_raw[...].astype(jnp.float32)
    kv[0, 0, rows : 2 * rows, :] = (k * cosine + pltpu.roll(k, HEAD // 2, 1) * sine).astype(jnp.bfloat16)
    for a in (2, 1):
        for d in range(2):
            if a <= far[d]:
                pass_on(d, a, 0, a).start()

    mine = pl.ds(pl.multiple_of(tp * slab, slab), slab)
    copies = []
    own = None
    for i in range(ntp):
        t = (tp + i) % ntp
        piece = grad_in.at[:, pl.ds(pl.multiple_of(t * width, width), width)]
        for a, where in enumerate((me, at_y)):
            if i == 0 and a == 0:
                own = pltpu.make_async_copy(piece, do_all.at[2, mine, :], local.at[5])
                own.start()
            else:
                slot = 2 if a == 0 else 0
                copies.append(
                    send(piece, do_all.at[slot, mine, :], do_send.at[a, i], do_recv.at[a, i], {"ctx": where, "tp": t})
                )
                copies[-1].start()

    loads[2].wait()
    for h in range(heads):
        at = slice(h * HEAD, (h + 1) * HEAD)
        x = q_raw[:, at].astype(jnp.float32)
        q_all[2, at, :] = (x * cosine + pltpu.roll(x, HEAD // 2, 1) * sine).astype(jnp.bfloat16)
    q_y = send(q_all.at[2], q_all.at[0], q_send.at[0], q_recv.at[0], y_peer)
    q_core = send(q_all.at[2], q_all.at[3], q_send.at[1], q_recv.at[1], core_peer)
    q_y.start()
    q_core.start()

    arrived(1)
    for a in range(2, near + 1):
        arrived(a)
    later = list(range(near + 1, half - 1))

    def from_slot(slot, axis, i):
        t = (tp - i + ntp) % ntp
        there = do_all.at[slot, pl.ds(pl.multiple_of(t * slab, slab), slab), :]
        return send(there, there, do_send.at[axis, i], do_recv.at[axis, i], core_peer)

    own.wait()
    for i in range(1, ntp):
        from_slot(2, 0, i).wait_recv()
    forward = [send(do_all.at[2], do_all.at[3], fwd_send.at[0], fwd_recv.at[0], core_peer)]
    forward[0].start()
    loads[3].wait()
    loads[4].wait()
    for h in range(heads):
        at = slice(h * HEAD, (h + 1) * HEAD)
        product = do_all[2, :, at].astype(jnp.float32) * out_raw[:, at].astype(jnp.float32)
        stats[2, 0, h : h + 1, :] = lse_raw[h : h + 1, :] * LOG2E
        stats[2, 1, h : h + 1, :] = jnp.sum(product.T, axis=0, keepdims=True)
    small = [
        send(stats.at[2], stats.at[slot], st_send.at[i], st_recv.at[i], peer)
        for i, (slot, peer) in enumerate(((3, core_peer), (0, y_peer), (1, cross_peer)))
    ]
    for copy in small:
        copy.start()
    q_y.wait_recv()
    forward.append(send(q_all.at[0], q_all.at[1], fwd_send.at[1], fwd_recv.at[1], core_peer))
    forward[1].start()
    if later:
        arrived(later[0])
    forward.append(send(do_all.at[0], do_all.at[1], fwd_send.at[2], fwd_recv.at[2], core_peer))
    for copy in (q_core, forward[0], small[0]):
        copy.wait_recv()

    sub = lax.broadcasted_iota(jnp.int32, (BLK, HEAD), 0)

    def unit(p, g):
        kp, vp = kv[p, 0], kv[p, 1]
        slots = (2 * g, 2 * g + 1)
        qs = jnp.concatenate([q_all[slot] for slot in slots], axis=0)
        grads = jnp.concatenate(
            [do_all[slot, :, h * HEAD : (h + 1) * HEAD] for slot in slots for h in range(heads)], axis=0
        )
        up = (p + half - 1) % half + 1
        shards_z = ((z + up) % nz, (z - p + nz) % nz)
        places = [map_in[(s * QUAD + j) * 2 + b] * BLK for s in shards_z for b in range(2)]
        s = lax.dot_general(kp, qs, (((1,), (1,)), ((), ())), preferred_element_type=jnp.float32)
        dp = lax.dot_general(vp, grads, (((1,), (1,)), ((), ())), preferred_element_type=jnp.float32)
        probs, scores = [], []
        for i, slot in enumerate(slots):
            bound = limits[slot]
            allowed = jnp.concatenate([sub <= bound - place for place in places], axis=0)
            for h in range(heads):
                at = slice((i * heads + h) * HEAD, (i * heads + h + 1) * HEAD)
                x = s[:, at] * (scale * LOG2E) - stats[slot, 0, h : h + 1, :]
                prob = jnp.exp2(jnp.where(allowed, x, -jnp.inf))
                probs.append(prob.astype(jnp.bfloat16))
                scores.append((prob * (dp[:, at] - stats[slot, 1, h : h + 1, :])).astype(jnp.bfloat16))
        probs = jnp.concatenate(probs, axis=1)
        scores = jnp.concatenate(scores, axis=1)
        dv = jnp.dot(probs, grads, preferred_element_type=jnp.float32)
        dk = jnp.dot(scores, qs, preferred_element_type=jnp.float32) * scale
        part[p, 0] += dk
        part[p, 1] += dv
        dq[g] += lax.dot_general(scores, kp, (((0,), (0,)), ((), ())), preferred_element_type=jnp.float32)

    def part_of(d, s, p):
        return part[p, :, (0 if d == 0 else rows) : (rows if d == 0 else 2 * rows), :]

    def give(d, s, source, places):
        return send(
            source, carry.at[d, s], rs_send.at[d, s], rs_recv.at[d, s], along[places if d == 0 else -places]
        )

    def start_chain(d, s, p, places):
        stage[d, s] = part_of(d, s, p).astype(jnp.bfloat16)
        give(d, s, stage.at[d, s], places).start()

    def add_and_give(d, s, p, places):
        give(d, s + 2, carry.at[d, s + 2], 1).wait_recv()
        carry[d, s + 2] = (carry[d, s + 2].astype(jnp.float32) + part_of(d, s, p)).astype(jnp.bfloat16)
        give(d, s, carry.at[d, s + 2], places).start()

    to_core = [send(dq_go.at[i], first.at[i], dq_send.at[i], dq_recv.at[i], core_peer) for i in range(2)]
    to_y = send(back, second, dq_send.at[2], dq_recv.at[2], y_peer)
    span_rows = heads * HEAD

    def one_unit(u, unused):
        late = (u + 2 * half - 2 * near) // (2 * half)
        last = (u + 4) // (2 * half)
        order = (u + 2 * half - 2 * near) % (2 * half) // 2
        order = (1 - last) * order + last * (half - near - 2 + u % 2)
        s = half - order
        p = (1 - late) * (u % near + 1) + late * (s % half)
        g = (1 - late) * (1 - u // near % 2) + late * ((1 - last) * (u % 2) + last * (u % 4 // 2))

        @pl.when(u == 2 * near)
        def _():
            pass_on(0, half, half, 1).wait_recv()

        if half - 1 > near:

            @pl.when(u == 2 * near + 2)
            def _():
                arrived(half - 1)

        unit(p, g)

        @pl.when(u == 0)
        def _():
            if len(later) > 1:
                arrived(later[1])
            for i in range(ntp):
                from_slot(0, 1, i).wait_recv()
            forward[2].start()

        if len(later) > 2:

            @pl.when(u == 1)
            def _():
                arrived(later[2])

        @pl.when(u == near - 1)
        def _():
            for copy in (*forward[1:], *small[1:]):
                copy.wait_recv()

        @pl.when(u == 2 * half - 3)
        def _():
            dq_go[0] = (dq[0, span_rows : 2 * span_rows, :] * scale).astype(jnp.bfloat16)
            to_core[0].start()

        for order_of in range(half - near):
            place = half - order_of
            ends = 2 * half - 2 + order_of - (half - near - 2)
            done = ends if order_of >= half - near - 2 else 2 * (near + order_of) + 1

            @pl.when(u == done)
            def _():
                for d in range(2):
                    places = 2 if place - 2 > near else place
                    if place + 2 <= far[d]:
                        add_and_give(d, place, place % half, places)
                    elif place <= far[d]:
                        start_chain(d, place, place % half, places)
                if order_of == 0:
                    for a in range(1, near + 1):
                        for d in range(2):
                            start_chain(d, a, a, a)

        @pl.when(u == 2 * half - 2)
        def _():
            to_core[0].wait_recv()
            back[...] = (dq[0, 0:span_rows, :] * scale + first[0].astype(jnp.float32)).astype(jnp.bfloat16)
            to_y.start()

        return unused

    lax.fori_loop(0, 2 * half, one_unit, 0)
    dq_go[1] = (dq[1, span_rows : 2 * span_rows, :] * scale).astype(jnp.bfloat16)
    to_core[1].start()
    to_core[1].wait_recv()
    ends = [part[0, what, rows : 2 * rows, :] for what in range(2)]
    for d in range(2):
        for s in range(1, near + 3):
            if s <= far[d]:
                give(d, s, carry.at[d, s], 1).wait_recv()
                ends = [ends[what] + carry[d, s, what].astype(jnp.float32) for what in range(2)]
    all_out[:, width : width + HEAD] = (ends[0] * cosine - pltpu.roll(ends[0], HEAD // 2, 1) * sine).astype(jnp.bfloat16)
    all_out[:, width + HEAD :] = ends[1].astype(jnp.bfloat16)
    to_y.wait_recv()
    for h in range(heads):
        at = slice(h * HEAD, (h + 1) * HEAD)
        x = dq[1, at, :] * scale + first[1, at, :].astype(jnp.float32) + second[at, :].astype(jnp.float32)
        all_out[:, at] = (x * cosine - pltpu.roll(x, HEAD // 2, 1) * sine).astype(jnp.bfloat16)

    for d in range(2):
        for a in range(1, far[d] + 1):
            pass_on(d, a, 0, 1).wait_send()
            give(d, a, stage.at[d, 0], 1).wait_send()
    for copy in (*copies, q_y, q_core, *forward, *small, *to_core, to_y):
        copy.wait_send()


def divide_kernel(together, gq_out, gk_out, gv_out, done):
    width = gq_out.shape[1]
    copies = [
        pltpu.make_async_copy(together.at[:, pl.ds(start, out.shape[1])], out, done.at[i])
        for i, (start, out) in enumerate(((0, gq_out), (width, gk_out), (width + HEAD, gv_out)))
    ]
    for copy in copies:
        copy.start()
    for copy in copies:
        copy.wait()


def shards(queries, keys, values, attn_out, out_grad, logsumexp, position_ids, block_map, span_blocks):
    rows, width = queries.shape
    heads = width // HEAD
    nz = lax.axis_size("ctx") // QUAD
    ntp = lax.axis_size("tp")
    vmem = pl.BlockSpec(memory_space=pltpu.VMEM)
    smem = pl.BlockSpec(memory_space=pltpu.SMEM)
    hbm = pl.BlockSpec(memory_space=pl.ANY)
    dma = pltpu.SemaphoreType.DMA
    bf16, f32 = jnp.bfloat16, jnp.float32
    half = nz // 2
    tall = heads * HEAD
    together = pl.pallas_call(
        functools.partial(step_kernel, nz, ntp),
        out_shape=jax.ShapeDtypeStruct((rows, width + 2 * HEAD), bf16),
        in_specs=[smem, smem, hbm, hbm, hbm, hbm, hbm, hbm, vmem],
        out_specs=vmem,
        scratch_shapes=[
            pltpu.VMEM((rows, width), bf16),
            pltpu.VMEM((rows, width), bf16),
            pltpu.VMEM((heads, rows), f32),
            pltpu.VMEM((rows, HEAD), bf16),
            pltpu.VMEM((QUAD, tall, HEAD), bf16),
            pltpu.VMEM((QUAD, rows, width), bf16),
            pltpu.VMEM((QUAD, 2, heads, rows), f32),
            pltpu.VMEM((half, 2, 2 * rows, HEAD), bf16),
            pltpu.VMEM((half, 2, 2 * rows, HEAD), f32),
            pltpu.VMEM((2, 2 * tall, HEAD), f32),
            pltpu.VMEM((2, tall, HEAD), bf16),
            pltpu.VMEM((2, tall, HEAD), bf16),
            pltpu.VMEM((tall, HEAD), bf16),
            pltpu.VMEM((2, half + 1, 2, rows, HEAD), bf16),
            pltpu.VMEM((2, half + 1, 2, rows, HEAD), bf16),
            pltpu.VMEM((tall, HEAD), bf16),
            pltpu.VMEM((QUAD, 1, HEAD), jnp.int32),
            dma((6,)), dma((2, ntp)), dma((2, ntp)), dma((2, half + 1)), dma((2, half + 1)),
            dma((2,)), dma((2,)), dma((3,)), dma((3,)), dma((3,)), dma((3,)),
            dma((2, half + 1)), dma((2, half + 1)), dma((3,)), dma((3,)),
        ],
        compiler_params=pltpu.CompilerParams(
            vmem_limit_bytes=56 * 1024 * 1024, collective_id=0, has_side_effects=True
        ),
        name="attention_backward",
    )(
        block_map, span_blocks.T, queries, keys, values, attn_out, out_grad, logsumexp, position_ids
    )
    return pl.pallas_call(
        divide_kernel,
        out_shape=(
            jax.ShapeDtypeStruct((rows, width), bf16),
            jax.ShapeDtypeStruct((rows, HEAD), bf16),
            jax.ShapeDtypeStruct((rows, HEAD), bf16),
        ),
        in_specs=[hbm],
        out_specs=(hbm, hbm, hbm),
        scratch_shapes=[dma((3,))],
        name="divide_result",
    )(together)


def solution(mesh):
    return jax.shard_map(
        shards,
        mesh=mesh,
        in_specs=(
            P("ctx", "tp"),
            P("ctx", "tp"),
            P("ctx", "tp"),
            P("ctx", "tp"),
            P(("ctx", "tp"), None),
            P("tp", "ctx"),
            P(None, "ctx"),
            P(),
            P(),
        ),
        out_specs=(P("ctx", "tp"), P("ctx", "tp"), P("ctx", "tp")),
        check_vma=False,
    )
```

```python
import functools
import math

import jax
import jax.numpy as jnp
from jax import lax
from jax.experimental import pallas as pl
from jax.experimental.pallas import tpu as pltpu
from jax.sharding import PartitionSpec as P

HEAD = 128
BLK = 64
QUAD = 4
THETA = 1000000.0
LOG2E = 1.4426950408889634


def rope_tables(ids):
    half = HEAD // 2
    pair = lax.broadcasted_iota(jnp.int32, (half, HEAD), 0)
    inverse = jnp.exp(pair.astype(jnp.float32) * jnp.float32(-2.0 * math.log(THETA) / HEAD))
    first_cut = HEAD // 8
    second_cut = first_cut + 3 * HEAD // 16
    picked = jnp.where(pair < first_cut, ids[0:1, :], jnp.where(pair < second_cut, ids[1:2, :], ids[2:3, :]))
    angles = picked.astype(jnp.float32) * inverse
    cosine, sine = jnp.cos(angles), jnp.sin(angles)
    return jnp.concatenate([cosine, cosine], axis=0).T, jnp.concatenate([-sine, sine], axis=0).T


MESH = pl.DeviceIdType.MESH


def signal_all(barrier, peers):
    for peer in peers:
        pl.semaphore_signal(barrier, inc=1, device_id=peer, device_id_type=MESH)


def send(source, target, send_sem, recv_sem, peer):
    return pltpu.make_async_remote_copy(
        src_ref=source,
        dst_ref=target,
        send_sem=send_sem,
        recv_sem=recv_sem,
        device_id=peer,
        device_id_type=MESH,
    )


def step_kernel(
    nz, ntp, map_in, span_in, q_in, k_in, v_in, out_in, grad_in, lse_in, ids_in,
    all_out,
    q_raw, out_raw, lse_raw, k_raw, q_all, do_all, stats, kv, part, dq, dq_go, first, second, carry, stage, back, limits,
    local, do_send, do_recv, kv_send, kv_recv, q_send, q_recv, fwd_send, fwd_recv, st_send, st_recv,
    rs_send, rs_recv, dq_send, dq_recv,
):
    me = lax.axis_index("ctx")
    tp = lax.axis_index("tp")
    z, j = me // QUAD, me % QUAD
    yh, core = j // 2, j % 2
    rows, width = q_in.shape
    heads = width // HEAD
    slab = rows // ntp
    n = nz * QUAD
    half = nz // 2
    far = (half, half - 1)
    scale = 1.0 / math.sqrt(HEAD)
    at_core = me + 1 - 2 * core
    at_y = me + 2 - 4 * yh
    core_peer = {"ctx": at_core, "tp": tp}
    y_peer = {"ctx": at_y, "tp": tp}
    cross_peer = {"ctx": at_core + 2 - 4 * yh, "tp": tp}
    near = 3 if half >= 8 else 2
    along = {k: {"ctx": (me + QUAD * k + n) % n, "tp": tp} for i in range(1, near + 2) for k in (i, -i)}

    loads = [
        pltpu.make_async_copy(source, target, local.at[i])
        for i, (source, target) in enumerate(
            ((k_in, k_raw), (v_in, kv.at[0, 1, pl.ds(rows, rows), :]), (q_in, q_raw), (out_in, out_raw), (lse_in, lse_raw))
        )
    ]
    for load in loads:
        load.start()
    others = [{"ctx": where, "tp": (tp + i) % ntp} for where in (me, at_y) for i in range(1, ntp)]
    peers = [*along.values(), core_peer, y_peer, cross_peer, *others]
    barrier = pltpu.get_barrier_semaphore()
    signal_all(barrier, peers)
    cosine, sine = rope_tables(ids_in)
    lane = lax.broadcasted_iota(jnp.int32, (1, HEAD), 1)
    dq[...] = jnp.zeros_like(dq)
    part[...] = jnp.zeros_like(part)

    def limit_of(block):
        place = map_in[block]
        end = jnp.int32(0)
        for i in range(span_in.shape[1]):
            inside = (place >= span_in[0, i]) & (place < span_in[1, i])
            end = end + jnp.where(inside, span_in[1, i], 0)
        return place * BLK, end * BLK - 1

    for slot, member in enumerate((j + 2 - 4 * yh, (j + 2 - 4 * yh) + 1 - 2 * core, j, j + 1 - 2 * core)):
        pieces = []
        for b in range(2):
            place, end = limit_of((z * QUAD + member) * 2 + b)
            pieces.append(jnp.maximum(place + lane - b * BLK, end))
        limits[slot] = jnp.where(lane < BLK, pieces[0], pieces[1])
    pl.semaphore_wait(barrier, len(peers))

    def shard(d, a):
        if a == 0 or a == half:
            return kv.at[0, :, pl.ds(rows if a == 0 else 0, rows), :]
        return kv.at[a, :, pl.ds(rows if d == 0 else 0, rows), :]

    def pass_on(d, a, from_a, places):
        return send(
            shard(d, from_a), shard(d, a), kv_send.at[d, a], kv_recv.at[d, a], along[places if d == 0 else -places]
        )

    def arrived(a):
        for d in range(2):
            if a <= far[d]:
                pass_on(d, a, a, 1).wait_recv()
            if a + 2 <= far[d]:
                pass_on(d, a + 2, a, 2).start()

    loads[0].wait()
    loads[1].wait()
    k = k_raw[...].astype(jnp.float32)
    kv[0, 0, rows : 2 * rows, :] = (k * cosine + pltpu.roll(k, HEAD // 2, 1) * sine).astype(jnp.bfloat16)
    for a in (2, 1):
        for d in range(2):
            if a <= far[d]:
                pass_on(d, a, 0, a).start()

    mine = pl.ds(pl.multiple_of(tp * slab, slab), slab)
    copies = []
    own = None
    for i in range(ntp):
        t = (tp + i) % ntp
        piece = grad_in.at[:, pl.ds(pl.multiple_of(t * width, width), width)]
        for a, where in enumerate((me, at_y)):
            if i == 0 and a == 0:
                own = pltpu.make_async_copy(piece, do_all.at[2, mine, :], local.at[5])
                own.start()
            else:
                slot = 2 if a == 0 else 0
                copies.append(
                    send(piece, do_all.at[slot, mine, :], do_send.at[a, i], do_recv.at[a, i], {"ctx": where, "tp": t})
                )
                copies[-1].start()

    loads[2].wait()
    for h in range(heads):
        at = slice(h * HEAD, (h + 1) * HEAD)
        x = q_raw[:, at].astype(jnp.float32)
        q_all[2, at, :] = (x * cosine + pltpu.roll(x, HEAD // 2, 1) * sine).astype(jnp.bfloat16)
    q_y = send(q_all.at[2], q_all.at[0], q_send.at[0], q_recv.at[0], y_peer)
    q_core = send(q_all.at[2], q_all.at[3], q_send.at[1], q_recv.at[1], core_peer)
    q_y.start()
    q_core.start()

    arrived(1)
    for a in range(2, near + 1):
        arrived(a)
    later = list(range(near + 1, half - 1))

    def from_slot(slot, axis, i):
        t = (tp - i + ntp) % ntp
        there = do_all.at[slot, pl.ds(pl.multiple_of(t * slab, slab), slab), :]
        return send(there, there, do_send.at[axis, i], do_recv.at[axis, i], core_peer)

    own.wait()
    for i in range(1, ntp):
        from_slot(2, 0, i).wait_recv()
    forward = [send(do_all.at[2], do_all.at[3], fwd_send.at[0], fwd_recv.at[0], core_peer)]
    forward[0].start()
    loads[3].wait()
    loads[4].wait()
    for h in range(heads):
        at = slice(h * HEAD, (h + 1) * HEAD)
        product = do_all[2, :, at].astype(jnp.float32) * out_raw[:, at].astype(jnp.float32)
        stats[2, 0, h : h + 1, :] = lse_raw[h : h + 1, :] * LOG2E
        stats[2, 1, h : h + 1, :] = jnp.sum(product.T, axis=0, keepdims=True)
    small = [
        send(stats.at[2], stats.at[slot], st_send.at[i], st_recv.at[i], peer)
        for i, (slot, peer) in enumerate(((3, core_peer), (0, y_peer), (1, cross_peer)))
    ]
    for copy in small:
        copy.start()
    q_y.wait_recv()
    forward.append(send(q_all.at[0], q_all.at[1], fwd_send.at[1], fwd_recv.at[1], core_peer))
    forward[1].start()
    if later:
        arrived(later[0])
    forward.append(send(do_all.at[0], do_all.at[1], fwd_send.at[2], fwd_recv.at[2], core_peer))
    for copy in (q_core, forward[0], small[0]):
        copy.wait_recv()

    sub = lax.broadcasted_iota(jnp.int32, (BLK, HEAD), 0)

    def unit(p, g):
        kp, vp = kv[p, 0], kv[p, 1]
        slots = (2 * g, 2 * g + 1)
        qs = jnp.concatenate([q_all[slot] for slot in slots], axis=0)
        grads = jnp.concatenate(
            [do_all[slot, :, h * HEAD : (h + 1) * HEAD] for slot in slots for h in range(heads)], axis=0
        )
        up = (p + half - 1) % half + 1
        shards_z = ((z + up) % nz, (z - p + nz) % nz)
        places = [map_in[(s * QUAD + j) * 2 + b] * BLK for s in shards_z for b in range(2)]
        s = lax.dot_general(kp, qs, (((1,), (1,)), ((), ())), preferred_element_type=jnp.float32)
        dp = lax.dot_general(vp, grads, (((1,), (1,)), ((), ())), preferred_element_type=jnp.float32)
        probs, scores = [], []
        for i, slot in enumerate(slots):
            bound = limits[slot]
            allowed = jnp.concatenate([sub <= bound - place for place in places], axis=0)
            for h in range(heads):
                at = slice((i * heads + h) * HEAD, (i * heads + h + 1) * HEAD)
                x = s[:, at] * (scale * LOG2E) - stats[slot, 0, h : h + 1, :]
                prob = jnp.exp2(jnp.where(allowed, x, -jnp.inf))
                probs.append(prob.astype(jnp.bfloat16))
                scores.append((prob * (dp[:, at] - stats[slot, 1, h : h + 1, :])).astype(jnp.bfloat16))
        probs = jnp.concatenate(probs, axis=1)
        scores = jnp.concatenate(scores, axis=1)
        dv = jnp.dot(probs, grads, preferred_element_type=jnp.float32)
        dk = jnp.dot(scores, qs, preferred_element_type=jnp.float32) * scale
        part[p, 0] += dk
        part[p, 1] += dv
        dq[g] += lax.dot_general(scores, kp, (((0,), (0,)), ((), ())), preferred_element_type=jnp.float32)

    def part_of(d, s, p):
        return part[p, :, (0 if d == 0 else rows) : (rows if d == 0 else 2 * rows), :]

    def give(d, s, source, places):
        return send(
            source, carry.at[d, s], rs_send.at[d, s], rs_recv.at[d, s], along[places if d == 0 else -places]
        )

    def start_chain(d, s, p, places):
        stage[d, s] = part_of(d, s, p).astype(jnp.bfloat16)
        give(d, s, stage.at[d, s], places).start()

    def add_and_give(d, s, p, places):
        give(d, s + 1, carry.at[d, s + 1], 1).wait_recv()
        carry[d, s + 1] = (carry[d, s + 1].astype(jnp.float32) + part_of(d, s, p)).astype(jnp.bfloat16)
        give(d, s, carry.at[d, s + 1], places).start()

    to_core = [send(dq_go.at[i], first.at[i], dq_send.at[i], dq_recv.at[i], core_peer) for i in range(2)]
    to_y = send(back, second, dq_send.at[2], dq_recv.at[2], y_peer)
    span_rows = heads * HEAD

    def one_unit(u, unused):
        late = (u + 2 * half - 2 * near) // (2 * half)
        order = (u + 2 * half - 2 * near) % (2 * half) // 2
        s = half - order
        p = (1 - late) * (u % near + 1) + late * (s % half)
        g = (1 - late) * (1 - u // near % 2) + late * (u % 2)

        @pl.when(u == 2 * near)
        def _():
            pass_on(0, half, half, 1).wait_recv()

        if half - 1 > near:

            @pl.when(u == 2 * near + 2)
            def _():
                arrived(half - 1)

        unit(p, g)

        @pl.when(u == 0)
        def _():
            if len(later) > 1:
                arrived(later[1])
            for i in range(ntp):
                from_slot(0, 1, i).wait_recv()
            forward[2].start()

        if len(later) > 2:

            @pl.when(u == 1)
            def _():
                arrived(later[2])

        @pl.when(u == near - 1)
        def _():
            for copy in (*forward[1:], *small[1:]):
                copy.wait_recv()

        @pl.when(u == 2 * half - 2)
        def _():
            dq_go[0] = (dq[0, span_rows : 2 * span_rows, :] * scale).astype(jnp.bfloat16)
            to_core[0].start()

        for order_of in range(half - near):
            place = half - order_of

            @pl.when(u == 2 * (near + order_of) + 1)
            def _():
                for d in range(2):
                    places = 1 if place - 1 > near else place
                    if place + 1 <= far[d]:
                        add_and_give(d, place, place % half, places)
                    elif place <= far[d]:
                        start_chain(d, place, place % half, places)
                if order_of == 0:
                    for a in range(1, near + 1):
                        for d in range(2):
                            start_chain(d, a, a, a)

        return unused

    lax.fori_loop(0, 2 * half, one_unit, 0)
    to_core[0].wait_recv()
    back[...] = (dq[0, 0:span_rows, :] * scale + first[0].astype(jnp.float32)).astype(jnp.bfloat16)
    to_y.start()
    dq_go[1] = (dq[1, span_rows : 2 * span_rows, :] * scale).astype(jnp.bfloat16)
    to_core[1].start()
    to_core[1].wait_recv()
    ends = [part[0, what, rows : 2 * rows, :] for what in range(2)]
    for d in range(2):
        for s in range(1, near + 2):
            if s <= far[d]:
                give(d, s, carry.at[d, s], 1).wait_recv()
                ends = [ends[what] + carry[d, s, what].astype(jnp.float32) for what in range(2)]
    all_out[:, width : width + HEAD] = (ends[0] * cosine - pltpu.roll(ends[0], HEAD // 2, 1) * sine).astype(jnp.bfloat16)
    all_out[:, width + HEAD :] = ends[1].astype(jnp.bfloat16)
    to_y.wait_recv()
    for h in range(heads):
        at = slice(h * HEAD, (h + 1) * HEAD)
        x = dq[1, at, :] * scale + first[1, at, :].astype(jnp.float32) + second[at, :].astype(jnp.float32)
        all_out[:, at] = (x * cosine - pltpu.roll(x, HEAD // 2, 1) * sine).astype(jnp.bfloat16)

    for d in range(2):
        for a in range(1, far[d] + 1):
            pass_on(d, a, 0, 1).wait_send()
            give(d, a, stage.at[d, 0], 1).wait_send()
    for copy in (*copies, q_y, q_core, *forward, *small, *to_core, to_y):
        copy.wait_send()


def shards(queries, keys, values, attn_out, out_grad, logsumexp, position_ids, block_map, span_blocks):
    rows, width = queries.shape
    heads = width // HEAD
    nz = lax.axis_size("ctx") // QUAD
    ntp = lax.axis_size("tp")
    vmem = pl.BlockSpec(memory_space=pltpu.VMEM)
    smem = pl.BlockSpec(memory_space=pltpu.SMEM)
    hbm = pl.BlockSpec(memory_space=pl.ANY)
    dma = pltpu.SemaphoreType.DMA
    bf16, f32 = jnp.bfloat16, jnp.float32
    half = nz // 2
    tall = heads * HEAD
    together = pl.pallas_call(
        functools.partial(step_kernel, nz, ntp),
        out_shape=jax.ShapeDtypeStruct((rows, width + 2 * HEAD), bf16),
        in_specs=[smem, smem, hbm, hbm, hbm, hbm, hbm, hbm, vmem],
        out_specs=vmem,
        scratch_shapes=[
            pltpu.VMEM((rows, width), bf16),
            pltpu.VMEM((rows, width), bf16),
            pltpu.VMEM((heads, rows), f32),
            pltpu.VMEM((rows, HEAD), bf16),
            pltpu.VMEM((QUAD, tall, HEAD), bf16),
            pltpu.VMEM((QUAD, rows, width), bf16),
            pltpu.VMEM((QUAD, 2, heads, rows), f32),
            pltpu.VMEM((half, 2, 2 * rows, HEAD), bf16),
            pltpu.VMEM((half, 2, 2 * rows, HEAD), f32),
            pltpu.VMEM((2, 2 * tall, HEAD), f32),
            pltpu.VMEM((2, tall, HEAD), bf16),
            pltpu.VMEM((2, tall, HEAD), bf16),
            pltpu.VMEM((tall, HEAD), bf16),
            pltpu.VMEM((2, half + 1, 2, rows, HEAD), bf16),
            pltpu.VMEM((2, half + 1, 2, rows, HEAD), bf16),
            pltpu.VMEM((tall, HEAD), bf16),
            pltpu.VMEM((QUAD, 1, HEAD), jnp.int32),
            dma((6,)), dma((2, ntp)), dma((2, ntp)), dma((2, half + 1)), dma((2, half + 1)),
            dma((2,)), dma((2,)), dma((3,)), dma((3,)), dma((3,)), dma((3,)),
            dma((2, half + 1)), dma((2, half + 1)), dma((3,)), dma((3,)),
        ],
        compiler_params=pltpu.CompilerParams(
            vmem_limit_bytes=56 * 1024 * 1024, collective_id=0, has_side_effects=True
        ),
        name="attention_backward",
    )(
        block_map, span_blocks.T, queries, keys, values, attn_out, out_grad, logsumexp, position_ids
    )
    return together[:, :width], together[:, width : width + HEAD], together[:, width + HEAD :]


def solution(mesh):
    return jax.shard_map(
        shards,
        mesh=mesh,
        in_specs=(
            P("ctx", "tp"),
            P("ctx", "tp"),
            P("ctx", "tp"),
            P("ctx", "tp"),
            P(("ctx", "tp"), None),
            P("tp", "ctx"),
            P(None, "ctx"),
            P(),
            P(),
        ),
        out_specs=(P("ctx", "tp"), P("ctx", "tp"), P("ctx", "tp")),
        check_vma=False,
    )
```
